32 devices in a mesh: grp: 2 (over y), row: 4 (over z), col: 2 (over x), half: 2 (over core).
Axes of the slice: x: 2, y: 2, z: 4, core: 2. Of those that a mesh axis runs over, the one named last changes fastest.
Arguments:
- vecs: bfloat16 [4, 1024, 32768], P(('grp', 'half'), 'row', 'col'), parts along dimension 0, may hold values from -6 to 6
- poles: float32 [4, 32768], P(('grp', 'half'), 'col'), parts along dimension 0, may hold values from -512 to 512, as said below
- weights: float32 [4, 32768], P(('grp', 'half'), 'col'), parts along dimension 0, may hold values from -5 to 5
- kept: int32 [4, 32768], P(('grp', 'half'), 'col'), parts along dimension 0, may hold values 0 or 1
- roots: float32 [1024], P(('grp', 'row')), parts along dimension 0, may hold values from -512 to 512, as said below
- order: int32 [1024], P('grp'), parts along dimension 0, may hold values from 0 to 511, each once
Outputs:
- merged: bfloat16 [16, 4, 2, 32, 512], P(('grp', 'row', 'half'), None, None, None, 'col'), parts along dimension 0
The draws below stay inside these ranges and needn't reach their ends.
There are 2 independent parts, one for each index of `grp`. The reference program is written for one: setup_inputs(seed, part) draws one part's arguments, and reference() takes and returns one part's arrays. A program takes and returns all parts, laid end to end along the dimension named above; each array names one. Nothing has to cross between parts.
Inputs may be any that keep to these rules, and one draw needn't show every extreme that they name: `poles`: every root differs from every pole by 0.2 or more. `roots`: every root differs from every pole by 0.2 or more. `order`: A permutation of 0 to 511.
All inputs are finite; a program needn't handle non-finite values. No bound on the sum of `kept` on one device may be relied on, other than what follows from the above.
Results may differ from the reference program's by a relative error of at most 0.0049.
Values may be sent and summed in bfloat16 or wider, within the bound.
No kernel may reach another device: no remote copies, remote signals or barrier semaphores. Data moves between devices by JAX's collectives and lax.ppermute only.
A program may use at most 64 MiB of HBM per device.

```python
import jax
import jax.numpy as jnp
from jax import lax

NH = 32768
PANEL = 512
BINS = 1024
QROWS = 1024
BS = 32
N_ROW = 4


def draw_poles(key, part):
    first = jax.random.fold_in(key, 11)
    second = jax.random.fold_in(key, 12)
    levels = jax.random.randint(first, (2, NH), -(BINS // 2), BINS // 2)
    frac = jax.random.uniform(second, (2, NH), jnp.float32, 0.0, 0.3)
    return levels.astype(jnp.float32) + frac


def draw_roots(key, part):
    first = jax.random.fold_in(key, 21)
    second = jax.random.fold_in(key, 22)
    levels = jax.random.randint(first, (PANEL,), -(BINS // 2), BINS // 2 - 1)
    frac = jax.random.uniform(second, (PANEL,), jnp.float32, 0.5, 0.8)
    return levels.astype(jnp.float32) + frac


def place_ends(drawn, stream_key, least, largest):
    extent = drawn.shape
    place = [jax.random.randint(jax.random.fold_in(stream_key, axis), (), 0, extent[axis]) for axis in range(len(extent))]
    drawn = drawn.at[tuple(place)].set(least)
    longest = extent.index(max(extent))
    place[longest] = (place[longest] + 1) % extent[longest]
    return drawn.at[tuple(place)].set(largest)


def shard_levels(key, extent, split, smallest, largest):
    loudness = 1.0
    for dim, blocks in split:
        draws = jax.random.uniform(jax.random.fold_in(jax.random.fold_in(key, 6), dim), (blocks,), jnp.float32, smallest / len(split), largest / len(split))
        loudness = loudness * jnp.repeat(jnp.exp(draws), extent[dim] // blocks).reshape((-1,) + (1,) * (len(extent) - 1 - dim))
    return loudness


def bell_draw(stream_key, dims, width, limit, shards=(), dtype=jnp.bfloat16):
    level = shard_levels(stream_key, dims, shards, -0.22, 0.18) if shards else 1.0
    drawn = jax.random.normal(stream_key, dims, jnp.float32) * width * level
    return jnp.minimum(jnp.maximum(drawn, -limit), limit).astype(dtype)


def setup_inputs(seed: int = 0, part: int = 0) -> dict:
    keys = jax.random.split(jax.random.key(seed), 7)
    part_splits = jax.random.split(jax.random.fold_in(keys[6], part), 7)
    return {
        "vecs": bell_draw(part_splits[0], (2, QROWS, NH), 1.0, 6.0, ((0, 2), (1, 4), (2, 2))),
        "poles": draw_poles(jax.random.fold_in(jax.random.fold_in(keys[6], part), 71), part),
        "weights": bell_draw(part_splits[2], (2, NH), 1.0, 5.0, ((0, 2), (1, 2)), jnp.float32),
        "kept": place_ends((jax.random.randint(part_splits[3], (2, NH), 0, 4) < 3).astype(jnp.int32), jax.random.fold_in(part_splits[3], 1), 0, 1),
        "roots": draw_roots(jax.random.fold_in(jax.random.fold_in(keys[6], part), 71), part),
        "order": jax.random.permutation(part_splits[5], PANEL).astype(jnp.int32),
    }


def reference(vecs, poles, weights, kept, roots, order):
    theta = roots[order.astype(jnp.int32)]
    scaled = weights * kept.astype(jnp.float32)
    cauchy = scaled[:, :, None] / (poles[:, :, None] - theta[None, None, :])
    norms = lax.optimization_barrier(jnp.sum(cauchy * cauchy, axis=(0, 1)))
    zpanel = (cauchy * lax.rsqrt(norms + 1e-06)).astype(jnp.bfloat16)
    upper = jnp.dot(vecs[0], zpanel[0], preferred_element_type=jnp.float32).astype(jnp.bfloat16)
    lower = jnp.dot(vecs[1], zpanel[1], preferred_element_type=jnp.float32).astype(jnp.bfloat16)
    product = jnp.stack([upper, lower], axis=0)
    blocks = product.reshape(2, N_ROW, 2 * N_ROW, BS, PANEL)
    return jnp.transpose(blocks, (2, 1, 0, 3, 4))
```

```python
import functools

import jax
import jax.numpy as jnp
from jax import lax
from jax.experimental import pallas as pl
from jax.experimental.pallas import tpu as pltpu
from jax.sharding import PartitionSpec as P

F32, BF16, I32 = jnp.float32, jnp.bfloat16, jnp.int32
LANES = 128
VMEM_BYTES = 67_043_328
SLACK = 32 << 10
TAIL = 8
VMEM = pl.BlockSpec(memory_space=pltpu.VMEM)


def params(mib):
    return pltpu.CompilerParams(vmem_limit_bytes=mib << 20)


def tile_of(size, most):
    tile = most
    while size % tile:
        tile //= 2
    return tile


def column_of(row):
    n = row.shape[1]
    sub = lax.broadcasted_iota(I32, (n, n), 0)
    lane = lax.broadcasted_iota(I32, (n, n), 1)
    return jnp.sum(jnp.where(sub == lane, row, jnp.zeros_like(row)), axis=1, keepdims=True)


def split(value):
    high = value.astype(BF16)
    return high, (value - high.astype(F32)).astype(BF16)


def norm_kernel(poles, weights, kept, roots, order, vecs, *refs):
    poles_in, roots_in, order_in, vecs_in, scaled, sums = refs[:6]
    weights_in, kept_in, acc, sem, bulk = refs[6:]
    pairs = ((poles, poles_in), (weights, weights_in), (kept, kept_in), (roots, roots_in), (order, order_in))
    small = [pltpu.make_async_copy(a, b, sem.at[i]) for i, (a, b) in enumerate(pairs)]
    for copy in small:
        copy.start()
    columns = poles.shape[1]
    chunks = bulk.shape[0]
    size = columns // chunks
    large = [
        pltpu.make_async_copy(
            vecs.at[0, :, i * size : (i + 1) * size], vecs_in.at[:, i * size : (i + 1) * size], bulk.at[i]
        )
        for i in range(chunks)
    ]
    for copy in large:
        copy.start()
    for copy in small:
        copy.wait()
    own = roots.shape[1]
    theta = jnp.broadcast_to(column_of(roots_in[...]), (own, LANES))
    acc[...] = jnp.zeros_like(acc)
    step = tile_of(columns, 4 * LANES)

    def body(i, carry):
        total = acc[...]
        for j in range(step // LANES):
            at = pl.ds(pl.multiple_of(i * step + j * LANES, LANES), LANES)
            s = weights_in[:, at] * kept_in[:, at].astype(F32)
            scaled[:, at] = s
            c = s * (1.0 / (poles_in[:, at] - theta))
            total = total + c * c
        acc[...] = total
        return carry

    lax.fori_loop(0, columns // step, body, 0)
    column = jnp.sum(acc[...], axis=1, keepdims=True)
    base = lax.axis_index("row") * own
    sub = lax.broadcasted_iota(I32, (own, order.shape[1]), 0)
    hit = (order_in[...] - base) == sub
    sums[...] = jnp.sum(jnp.where(hit, column, 0.0), axis=0, keepdims=True)
    for copy in large:
        copy.wait()


def panel_kernel(count, shift, *refs):
    roots = refs[:count]
    order, poles, scaled, vecs, sums, out, theta, panel, acc = refs[count:]
    nrows = vecs.shape[0]
    share = theta.shape[0]
    own = roots[0].shape[1]
    columns = poles.shape[1]
    me = lax.axis_index("row")
    cols = order.shape[1] // share
    target = lax.rem(lax.axis_index("col") + shift, cols)
    start = pl.multiple_of(target * share, LANES)
    for b in range(share // LANES):
        picks = column_of(order[:, pl.ds(pl.multiple_of(start + b * LANES, LANES), LANES)])
        total = jnp.zeros((LANES, own), F32)
        for s in range(count):
            base = partner(me, s, count) * own
            lane = lax.broadcasted_iota(I32, (LANES, own), 1) + base
            total = total + jnp.where(picks == lane, roots[s][...], 0.0)
        theta[b * LANES : (b + 1) * LANES, :] = jnp.broadcast_to(
            jnp.sum(total, axis=1, keepdims=True), (LANES, LANES)
        )

    block = tile_of(columns, 2048)
    tiles = block // LANES
    blocks = columns // block

    def make(slot, offset):
        for j in range(tiles):
            at = pl.ds(pl.multiple_of(offset + j * LANES, LANES), LANES)
            panel[slot, j] = (scaled[:, at] * (1.0 / (poles[:, at] - theta[...]))).astype(BF16)

    def product(slot, offset):
        left = jnp.concatenate([panel[slot, j] for j in range(tiles)], axis=1)
        right = vecs[:, pl.ds(pl.multiple_of(offset, block), block)]
        return lax.dot_general(left, right, (((1,), (1,)), ((), ())), preferred_element_type=F32)

    make(0, 0)
    acc[...] = jnp.zeros_like(acc)
    pairs = (blocks - 1) // 2

    def body(i, carry):
        offset = i * (2 * block)
        make(1, offset + block)
        acc[...] += product(0, offset)
        make(0, offset + 2 * block)
        acc[...] += product(1, offset + block)
        return carry

    lax.fori_loop(0, pairs, body, 0)
    at = pairs * 2
    if at + 1 < blocks:
        make(1, (at + 1) * block)
        acc[...] += product(0, at * block)
        at += 1
    total = acc[...] + product(at % 2, at * block)
    if shift == 0:
        out[...] = total
        return
    out[:nrows, :] = total.astype(BF16).T
    out[nrows:, :] = tail_rows(sums[:, pl.ds(start, share)], share)


def add_kernel(groups, product, sums, *refs):
    received, outs, full = refs[:-4], refs[-4:-1], refs[-1]
    share, nrows = product.shape
    norms = sums[:, pl.ds(pl.multiple_of(lax.axis_index("col") * share, LANES), share)]
    full[...] = product[...].T
    for ref in received:
        full[...] += ref[:nrows, :].astype(F32)
        norms = norms + ref[nrows : nrows + 1, :].astype(F32) + ref[nrows + 1 : nrows + 2, :].astype(F32)
    mine, other, total_norms = outs
    depth = nrows // groups
    half = lax.axis_index("half")
    for r in range(groups // 2):
        for which, ref in ((half, mine), (1 - half, other)):
            rows = pl.ds(pl.multiple_of((2 * r + which) * depth, depth), depth)
            ref[r * depth : (r + 1) * depth, :] = full[rows, :].astype(BF16)
    other[(groups // 2) * depth :, :] = tail_rows(norms, share)
    total_norms[...] = norms


def tail_rows(norms, share):
    high, low = split(norms)
    return jnp.concatenate([high, low, jnp.zeros((TAIL - 2, share), BF16)], axis=0)


def partner(index, step, size):
    if size & (size - 1) == 0:
        return index ^ step
    return lax.rem(index + size - step, size)


def exchange(value, axis, step):
    size = lax.axis_size(axis)
    pairs = [
        ((i ^ step) if size & (size - 1) == 0 else (i + size - step) % size, i) for i in range(size)
    ]
    return lax.ppermute(value, axis, pairs)


def message_kernel(count, depth, mine, got, norms, *outs):
    half = lax.axis_index("half")
    me = lax.axis_index("row")
    rows = count * depth
    share = mine.shape[1]
    total = norms[...] + got[rows : rows + 1, :].astype(F32) + got[rows + 1 : rows + 2, :].astype(F32)
    outs[-1][...] = total
    for s in range(count):
        at = pl.ds(pl.multiple_of(destination(me, s, count) * depth, depth), depth)
        first, second = mine[at, :], got[at, :]
        swap = half == 1
        out = outs[s]
        out[:depth, :] = jnp.where(swap, second, first)
        out[depth : 2 * depth, :] = jnp.where(swap, first, second)
        if s:
            out[2 * depth :, :] = tail_rows(total, share)


def destination(index, step, size):
    if size & (size - 1) == 0:
        return index ^ step
    return lax.rem(index + step, size)


def scale_kernel(count, depth, *refs):
    pieces, norms, out = refs[:count], refs[count], refs[count + 1]
    me = lax.axis_index("row")
    total = norms[...]
    for s in range(1, count):
        total = total + pieces[s][2 * depth : 2 * depth + 1, :].astype(F32)
        total = total + pieces[s][2 * depth + 1 : 2 * depth + 2, :].astype(F32)
    scale = lax.rsqrt(total + 1e-06)
    for s in range(count):
        value = (pieces[s][: 2 * depth, :].astype(F32) * scale).astype(BF16)
        out[partner(me, s, count)] = value


def body(vecs, poles, weights, kept, roots, order):
    row_count, col_count, halves = (lax.axis_size(a) for a in ("row", "col", "half"))
    own = roots.shape[0]
    width = order.shape[0]
    columns = poles.shape[1]
    nrows = vecs.shape[1]
    share = width // col_count
    groups = row_count * halves
    depth = nrows // groups
    direct = halves == 2 and depth % 16 == 0

    roots = roots.reshape(1, own)
    order = order.reshape(1, width)
    pieces = [roots] + [exchange(roots, "row", s) for s in range(1, row_count)]
    hbm = pl.BlockSpec(memory_space=pltpu.HBM)
    kept_bytes = 2 * nrows * columns + 4 * (2 * columns + own * row_count + 2 * width) + SLACK
    poles, roots_in, order, vecs, scaled, sums = pl.pallas_call(
        norm_kernel,
        out_shape=(
            pltpu.VMEM((1, columns), F32),
            pltpu.VMEM((1, own), F32),
            pltpu.VMEM((1, width), I32),
            pltpu.VMEM((nrows, columns), BF16),
            pltpu.VMEM((1, columns), F32),
            pltpu.VMEM((1, width), F32),
        ),
        in_specs=[hbm] * 6,
        out_specs=(VMEM,) * 6,
        scratch_shapes=[
            pltpu.VMEM((1, columns), F32),
            pltpu.VMEM((1, columns), I32),
            pltpu.VMEM((own, LANES), F32),
            pltpu.SemaphoreType.DMA((5,)),
            pltpu.SemaphoreType.DMA((8,)),
        ],
        compiler_params=pltpu.CompilerParams(vmem_limit_bytes=VMEM_BYTES - kept_bytes),
        cost_estimate=pl.CostEstimate(
            flops=6 * own * columns, transcendentals=own * columns, bytes_accessed=2 * nrows * columns
        ),
        name="norms",
    )(poles, weights, kept, roots, order, vecs)
    pieces[0] = roots_in
    block = tile_of(columns, 2048)

    def panel(shift):
        args = (*pieces, order, poles, scaled, vecs, sums)
        return pl.pallas_call(
            functools.partial(panel_kernel, row_count, shift),
            out_shape=pltpu.VMEM((nrows + TAIL, share), BF16) if shift else pltpu.VMEM((share, nrows), F32),
            in_specs=[VMEM] * len(args),
            out_specs=VMEM,
            scratch_shapes=[
                pltpu.VMEM((share, LANES), F32),
                pltpu.VMEM((2, block // LANES, share, LANES), BF16),
                pltpu.VMEM((share, nrows), F32),
            ],
            compiler_params=params(16),
            cost_estimate=pl.CostEstimate(
                flops=2 * share * nrows * columns,
                transcendentals=share * columns,
                bytes_accessed=nrows * columns * 2,
            ),
            name=f"panel_{shift}",
        )(*args)

    received = []
    for shift in range(1, col_count):
        pairs = [(i, (i + shift) % col_count) for i in range(col_count)]
        received.append(lax.ppermute(panel(shift), "col", pairs))
    product = panel(0)
    if not direct:
        full = jnp.transpose(product)
        norms = lax.dynamic_slice_in_dim(sums, lax.axis_index("col") * share, share, 1)
        for message in received:
            full = full + message[:nrows].astype(F32)
            norms = norms + jnp.sum(message[nrows : nrows + 2].astype(F32), axis=0, keepdims=True)
        norms = lax.psum(norms, ("row", "half"))
        moved = lax.all_to_all(
            full.astype(BF16).reshape(groups, depth, share),
            ("row", "half"),
            split_axis=0,
            concat_axis=0,
            tiled=True,
        )
        out = (moved.astype(F32) * lax.rsqrt(norms + 1e-06)).astype(BF16)
        return out.reshape(1, row_count, halves, depth, share)

    mine, other, norms = pl.pallas_call(
        functools.partial(add_kernel, groups),
        out_shape=(
            pltpu.VMEM((nrows // 2, share), BF16),
            pltpu.VMEM((nrows // 2 + TAIL, share), BF16),
            pltpu.VMEM((1, share), F32),
        ),
        in_specs=[VMEM] * (2 + len(received)),
        out_specs=(VMEM,) * 3,
        scratch_shapes=[pltpu.VMEM((nrows, share), F32)],
        compiler_params=params(4),
        name="add",
    )(product, sums, *received)
    got = exchange(other, "half", 1)
    shapes = [pltpu.VMEM((2 * depth + (TAIL if s else 0), share), BF16) for s in range(row_count)]
    *messages, norms = pl.pallas_call(
        functools.partial(message_kernel, row_count, depth),
        out_shape=(*shapes, pltpu.VMEM((1, share), F32)),
        in_specs=[VMEM] * 3,
        out_specs=(VMEM,) * (row_count + 1),
        compiler_params=params(4),
        name="messages",
    )(mine, got, norms)
    landed = [messages[0]]
    for s in range(1, row_count):
        pairs = [(i, destination_of(i, s, row_count)) for i in range(row_count)]
        landed.append(lax.ppermute(messages[s], "row", pairs))
    out = pl.pallas_call(
        functools.partial(scale_kernel, row_count, depth),
        out_shape=jax.ShapeDtypeStruct((row_count, 2 * depth, share), BF16),
        in_specs=[VMEM] * (row_count + 1),
        out_specs=VMEM,
        compiler_params=params(4),
        name="scale",
    )(*landed, norms)
    return out.reshape(1, row_count, halves, depth, share)


def destination_of(index, step, size):
    return (index ^ step) if size & (size - 1) == 0 else (index + step) % size


def solution(mesh):
    return jax.shard_map(
        body,
        mesh=mesh,
        in_specs=(
            P(("grp", "half"), "row", "col"),
            P(("grp", "half"), "col"),
            P(("grp", "half"), "col"),
            P(("grp", "half"), "col"),
            P(("grp", "row")),
            P("grp"),
        ),
        out_specs=P(("grp", "row", "half"), None, None, None, "col"),
        check_vma=False,
    )
```

```python
import functools

import jax
import jax.numpy as jnp
from jax import lax
from jax.experimental import pallas as pl
from jax.experimental.pallas import tpu as pltpu
from jax.sharding import PartitionSpec as P

F32, BF16, I32 = jnp.float32, jnp.bfloat16, jnp.int32
LANES = 128
VMEM_BYTES = 67_043_328
SLACK = 32 << 10
TAIL = 8
VMEM = pl.BlockSpec(memory_space=pltpu.VMEM)


def params(mib):
    return pltpu.CompilerParams(vmem_limit_bytes=mib << 20)


def tile_of(size, most):
    tile = most
    while size % tile:
        tile //= 2
    return tile


def column_of(row):
    n = row.shape[1]
    sub = lax.broadcasted_iota(I32, (n, n), 0)
    lane = lax.broadcasted_iota(I32, (n, n), 1)
    return jnp.sum(jnp.where(sub == lane, row, jnp.zeros_like(row)), axis=1, keepdims=True)


def split(value):
    high = value.astype(BF16)
    return high, (value - high.astype(F32)).astype(BF16)


def norm_kernel(poles, weights, kept, roots, order, vecs, *refs):
    poles_in, roots_in, order_in, vecs_in, scaled, sums = refs[:6]
    weights_in, kept_in, acc, sem, bulk = refs[6:]
    pairs = ((poles, poles_in), (weights, weights_in), (kept, kept_in), (roots, roots_in), (order, order_in))
    small = [pltpu.make_async_copy(a, b, sem.at[i]) for i, (a, b) in enumerate(pairs)]
    for copy in small:
        copy.start()
    columns = poles.shape[1]
    chunks = bulk.shape[0]
    size = columns // chunks
    large = [
        pltpu.make_async_copy(
            vecs.at[0, :, i * size : (i + 1) * size], vecs_in.at[:, i * size : (i + 1) * size], bulk.at[i]
        )
        for i in range(chunks)
    ]
    for copy in large:
        copy.start()
    for copy in small:
        copy.wait()
    own = roots.shape[1]
    theta = jnp.broadcast_to(column_of(roots_in[...]), (own, LANES))
    acc[...] = jnp.zeros_like(acc)
    step = tile_of(columns, 16 * LANES)

    def body(i, carry):
        total = acc[...]
        for j in range(step // LANES):
            at = pl.ds(pl.multiple_of(i * step + j * LANES, LANES), LANES)
            s = weights_in[:, at] * kept_in[:, at].astype(F32)
            scaled[:, at] = s
            c = s * (1.0 / (poles_in[:, at] - theta))
            total = total + c * c
        acc[...] = total
        return carry

    lax.fori_loop(0, columns // step, body, 0)
    column = jnp.sum(acc[...], axis=1, keepdims=True)
    base = lax.axis_index("row") * own
    sub = lax.broadcasted_iota(I32, (own, order.shape[1]), 0)
    hit = (order_in[...] - base) == sub
    sums[...] = jnp.sum(jnp.where(hit, column, 0.0), axis=0, keepdims=True)
    for copy in large:
        copy.wait()


def panel_kernel(count, shift, *refs):
    roots = refs[:count]
    order, poles, scaled, vecs, sums, out, theta, panel, acc = refs[count:]
    nrows = vecs.shape[0]
    share = theta.shape[0]
    own = roots[0].shape[1]
    columns = poles.shape[1]
    me = lax.axis_index("row")
    cols = order.shape[1] // share
    target = lax.rem(lax.axis_index("col") + shift, cols)
    start = pl.multiple_of(target * share, LANES)
    for b in range(share // LANES):
        picks = column_of(order[:, pl.ds(pl.multiple_of(start + b * LANES, LANES), LANES)])
        total = jnp.zeros((LANES, own), F32)
        for s in range(count):
            base = partner(me, s, count) * own
            lane = lax.broadcasted_iota(I32, (LANES, own), 1) + base
            total = total + jnp.where(picks == lane, roots[s][...], 0.0)
        theta[b * LANES : (b + 1) * LANES, :] = jnp.broadcast_to(
            jnp.sum(total, axis=1, keepdims=True), (LANES, LANES)
        )

    block = tile_of(columns, 2048)
    tiles = block // LANES
    blocks = columns // block

    def make(slot, offset):
        for j in range(tiles):
            at = pl.ds(pl.multiple_of(offset + j * LANES, LANES), LANES)
            panel[slot, j] = (scaled[:, at] * (1.0 / (poles[:, at] - theta[...]))).astype(BF16)

    def product(slot, offset):
        left = jnp.concatenate([panel[slot, j] for j in range(tiles)], axis=1)
        right = vecs[:, pl.ds(pl.multiple_of(offset, block), block)]
        return lax.dot_general(left, right, (((1,), (1,)), ((), ())), preferred_element_type=F32)

    make(0, 0)
    acc[...] = jnp.zeros_like(acc)
    pairs = (blocks - 1) // 2

    def body(i, carry):
        offset = i * (2 * block)
        make(1, offset + block)
        acc[...] += product(0, offset)
        make(0, offset + 2 * block)
        acc[...] += product(1, offset + block)
        return carry

    lax.fori_loop(0, pairs, body, 0)
    at = pairs * 2
    if at + 1 < blocks:
        make(1, (at + 1) * block)
        acc[...] += product(0, at * block)
        at += 1
    total = acc[...] + product(at % 2, at * block)
    if shift == 0:
        out[...] = total
        return
    out[:nrows, :] = total.astype(BF16).T
    out[nrows:, :] = tail_rows(sums[:, pl.ds(start, share)], share)


def add_kernel(groups, product, sums, *refs):
    received, outs, full = refs[:-4], refs[-4:-1], refs[-1]
    share, nrows = product.shape
    norms = sums[:, pl.ds(pl.multiple_of(lax.axis_index("col") * share, LANES), share)]
    full[...] = product[...].T
    for ref in received:
        full[...] += ref[:nrows, :].astype(F32)
        norms = norms + ref[nrows : nrows + 1, :].astype(F32) + ref[nrows + 1 : nrows + 2, :].astype(F32)
    mine, other, total_norms = outs
    depth = nrows // groups
    half = lax.axis_index("half")
    for r in range(groups // 2):
        for which, ref in ((half, mine), (1 - half, other)):
            rows = pl.ds(pl.multiple_of((2 * r + which) * depth, depth), depth)
            ref[r * depth : (r + 1) * depth, :] = full[rows, :].astype(BF16)
    other[(groups // 2) * depth :, :] = tail_rows(norms, share)
    total_norms[...] = norms


def tail_rows(norms, share):
    high, low = split(norms)
    return jnp.concatenate([high, low, jnp.zeros((TAIL - 2, share), BF16)], axis=0)


def partner(index, step, size):
    if size & (size - 1) == 0:
        return index ^ step
    return lax.rem(index + size - step, size)


def exchange(value, axis, step):
    size = lax.axis_size(axis)
    pairs = [
        ((i ^ step) if size & (size - 1) == 0 else (i + size - step) % size, i) for i in range(size)
    ]
    return lax.ppermute(value, axis, pairs)


def message_kernel(count, depth, mine, got, norms, *outs):
    half = lax.axis_index("half")
    me = lax.axis_index("row")
    rows = count * depth
    share = mine.shape[1]
    total = norms[...] + got[rows : rows + 1, :].astype(F32) + got[rows + 1 : rows + 2, :].astype(F32)
    outs[-1][...] = total
    for s in range(count):
        at = pl.ds(pl.multiple_of(destination(me, s, count) * depth, depth), depth)
        first, second = mine[at, :], got[at, :]
        swap = half == 1
        out = outs[count - 1 - s]
        out[:depth, :] = jnp.where(swap, second, first)
        out[depth : 2 * depth, :] = jnp.where(swap, first, second)
        if s:
            out[2 * depth :, :] = tail_rows(total, share)


def destination(index, step, size):
    if size & (size - 1) == 0:
        return index ^ step
    return lax.rem(index + step, size)


def scale_kernel(count, depth, *refs):
    pieces, norms, out = refs[:count][::-1], refs[count], refs[count + 1]
    me = lax.axis_index("row")
    total = norms[...]
    for s in range(1, count):
        total = total + pieces[s][2 * depth : 2 * depth + 1, :].astype(F32)
        total = total + pieces[s][2 * depth + 1 : 2 * depth + 2, :].astype(F32)
    scale = lax.rsqrt(total + 1e-06)
    for s in range(count):
        value = (pieces[s][: 2 * depth, :].astype(F32) * scale).astype(BF16)
        out[partner(me, s, count)] = value


def body(vecs, poles, weights, kept, roots, order):
    row_count, col_count, halves = (lax.axis_size(a) for a in ("row", "col", "half"))
    own = roots.shape[0]
    width = order.shape[0]
    columns = poles.shape[1]
    nrows = vecs.shape[1]
    share = width // col_count
    groups = row_count * halves
    depth = nrows // groups
    direct = halves == 2 and depth % 16 == 0

    roots = roots.reshape(1, own)
    order = order.reshape(1, width)
    pieces = [roots] + [exchange(roots, "row", s) for s in range(1, row_count)]
    hbm = pl.BlockSpec(memory_space=pltpu.HBM)
    kept_bytes = 2 * nrows * columns + 4 * (2 * columns + own * row_count + 2 * width) + SLACK
    poles, roots_in, order, vecs, scaled, sums = pl.pallas_call(
        norm_kernel,
        out_shape=(
            pltpu.VMEM((1, columns), F32),
            pltpu.VMEM((1, own), F32),
            pltpu.VMEM((1, width), I32),
            pltpu.VMEM((nrows, columns), BF16),
            pltpu.VMEM((1, columns), F32),
            pltpu.VMEM((1, width), F32),
        ),
        in_specs=[hbm] * 6,
        out_specs=(VMEM,) * 6,
        scratch_shapes=[
            pltpu.VMEM((1, columns), F32),
            pltpu.VMEM((1, columns), I32),
            pltpu.VMEM((own, LANES), F32),
            pltpu.SemaphoreType.DMA((5,)),
            pltpu.SemaphoreType.DMA((8,)),
        ],
        compiler_params=pltpu.CompilerParams(vmem_limit_bytes=VMEM_BYTES - kept_bytes),
        cost_estimate=pl.CostEstimate(
            flops=6 * own * columns, transcendentals=own * columns, bytes_accessed=2 * nrows * columns
        ),
        name="norms",
    )(poles, weights, kept, roots, order, vecs)
    pieces[0] = roots_in
    block = tile_of(columns, 2048)

    def panel(shift):
        args = (*pieces, order, poles, scaled, vecs, sums)
        return pl.pallas_call(
            functools.partial(panel_kernel, row_count, shift),
            out_shape=pltpu.VMEM((nrows + TAIL, share), BF16) if shift else pltpu.VMEM((share, nrows), F32),
            in_specs=[VMEM] * len(args),
            out_specs=VMEM,
            scratch_shapes=[
                pltpu.VMEM((share, LANES), F32),
                pltpu.VMEM((2, block // LANES, share, LANES), BF16),
                pltpu.VMEM((share, nrows), F32),
            ],
            compiler_params=params(16),
            cost_estimate=pl.CostEstimate(
                flops=2 * share * nrows * columns,
                transcendentals=share * columns,
                bytes_accessed=nrows * columns * 2,
            ),
            name=f"panel_{shift}",
        )(*args)

    received = []
    for shift in range(1, col_count):
        pairs = [(i, (i + shift) % col_count) for i in range(col_count)]
        received.append(lax.ppermute(panel(shift), "col", pairs))
    product = panel(0)
    if not direct:
        full = jnp.transpose(product)
        norms = lax.dynamic_slice_in_dim(sums, lax.axis_index("col") * share, share, 1)
        for message in received:
            full = full + message[:nrows].astype(F32)
            norms = norms + jnp.sum(message[nrows : nrows + 2].astype(F32), axis=0, keepdims=True)
        norms = lax.psum(norms, ("row", "half"))
        moved = lax.all_to_all(
            full.astype(BF16).reshape(groups, depth, share),
            ("row", "half"),
            split_axis=0,
            concat_axis=0,
            tiled=True,
        )
        out = (moved.astype(F32) * lax.rsqrt(norms + 1e-06)).astype(BF16)
        return out.reshape(1, row_count, halves, depth, share)

    mine, other, norms = pl.pallas_call(
        functools.partial(add_kernel, groups),
        out_shape=(
            pltpu.VMEM((nrows // 2, share), BF16),
            pltpu.VMEM((nrows // 2 + TAIL, share), BF16),
            pltpu.VMEM((1, share), F32),
        ),
        in_specs=[VMEM] * (2 + len(received)),
        out_specs=(VMEM,) * 3,
        scratch_shapes=[pltpu.VMEM((nrows, share), F32)],
        compiler_params=params(4),
        name="add",
    )(product, sums, *received)
    got = exchange(other, "half", 1)
    shapes = [pltpu.VMEM((2 * depth + (TAIL if s else 0), share), BF16) for s in range(row_count - 1, -1, -1)]
    *messages, norms = pl.pallas_call(
        functools.partial(message_kernel, row_count, depth),
        out_shape=(*shapes, pltpu.VMEM((1, share), F32)),
        in_specs=[VMEM] * 3,
        out_specs=(VMEM,) * (row_count + 1),
        compiler_params=params(4),
        name="messages",
    )(mine, got, norms)
    landed = []
    for s in range(row_count - 1, 0, -1):
        pairs = [(i, destination_of(i, s, row_count)) for i in range(row_count)]
        landed.append(lax.ppermute(messages[row_count - 1 - s], "row", pairs))
    landed.append(messages[-1])
    out = pl.pallas_call(
        functools.partial(scale_kernel, row_count, depth),
        out_shape=jax.ShapeDtypeStruct((row_count, 2 * depth, share), BF16),
        in_specs=[VMEM] * (row_count + 1),
        out_specs=VMEM,
        compiler_params=params(4),
        name="scale",
    )(*landed, norms)
    return out.reshape(1, row_count, halves, depth, share)


def destination_of(index, step, size):
    return (index ^ step) if size & (size - 1) == 0 else (index + step) % size


def solution(mesh):
    return jax.shard_map(
        body,
        mesh=mesh,
        in_specs=(
            P(("grp", "half"), "row", "col"),
            P(("grp", "half"), "col"),
            P(("grp", "half"), "col"),
            P(("grp", "half"), "col"),
            P(("grp", "row")),
            P("grp"),
        ),
        out_specs=P(("grp", "row", "half"), None, None, None, "col"),
        check_vma=False,
    )
```

```python
import functools

import jax
import jax.numpy as jnp
from jax import lax
from jax.experimental import pallas as pl
from jax.experimental.pallas import tpu as pltpu
from jax.sharding import PartitionSpec as P

F32, BF16, I32 = jnp.float32, jnp.bfloat16, jnp.int32
LANES = 128
VMEM_BYTES = 67_043_328
SLACK = 32 << 10
TAIL = 8
VMEM = pl.BlockSpec(memory_space=pltpu.VMEM)


def params(mib):
    return pltpu.CompilerParams(vmem_limit_bytes=mib << 20)


def tile_of(size, most):
    tile = most
    while size % tile:
        tile //= 2
    return tile


def column_of(row):
    n = row.shape[1]
    sub = lax.broadcasted_iota(I32, (n, n), 0)
    lane = lax.broadcasted_iota(I32, (n, n), 1)
    return jnp.sum(jnp.where(sub == lane, row, jnp.zeros_like(row)), axis=1, keepdims=True)


def split(value):
    high = value.astype(BF16)
    return high, (value - high.astype(F32)).astype(BF16)


def half_of(which, source, target, sem):
    parts = sem.shape[0]
    size = target.shape[1] // (2 * parts)
    spans = [slice((which * parts + i) * size, (which * parts + i + 1) * size) for i in range(parts)]
    return [
        pltpu.make_async_copy(source.at[0, :, at], target.at[:, at], sem.at[i]) for i, at in enumerate(spans)
    ]


def norm_kernel(poles, weights, kept, roots, order, vecs, *refs):
    poles_in, roots_in, order_in, vecs_in, scaled, sums = refs[:6]
    weights_in, kept_in, acc, sem, bulk = refs[6:]
    pairs = ((poles, poles_in), (weights, weights_in), (kept, kept_in), (roots, roots_in), (order, order_in))
    small = [pltpu.make_async_copy(a, b, sem.at[i]) for i, (a, b) in enumerate(pairs)]
    for copy in small:
        copy.start()
    columns = poles.shape[1]
    large = half_of(0, vecs, vecs_in, bulk)
    for copy in large:
        copy.start()
    for copy in small:
        copy.wait()
    own = roots.shape[1]
    theta = jnp.broadcast_to(column_of(roots_in[...]), (own, LANES))
    acc[...] = jnp.zeros_like(acc)
    step = tile_of(columns, 16 * LANES)

    def body(i, carry):
        total = acc[...]
        for j in range(step // LANES):
            at = pl.ds(pl.multiple_of(i * step + j * LANES, LANES), LANES)
            s = weights_in[:, at] * kept_in[:, at].astype(F32)
            scaled[:, at] = s
            c = s * (1.0 / (poles_in[:, at] - theta))
            total = total + c * c
        acc[...] = total
        return carry

    lax.fori_loop(0, columns // step, body, 0)
    column = jnp.sum(acc[...], axis=1, keepdims=True)
    base = lax.axis_index("row") * own
    sub = lax.broadcasted_iota(I32, (own, order.shape[1]), 0)
    hit = (order_in[...] - base) == sub
    sums[...] = jnp.sum(jnp.where(hit, column, 0.0), axis=0, keepdims=True)
    for copy in large:
        copy.wait()


def panel_kernel(count, shift, loads, *refs):
    roots = refs[:count]
    if loads:
        order, poles, scaled, sums, _, source, out, vecs, theta, panel, acc, sem = refs[count:]
        copies = half_of(1, source, vecs, sem)
        for copy in copies:
            copy.start()
    else:
        order, poles, scaled, sums, vecs, out, theta, panel, acc = refs[count:]
        copies = []
    nrows = vecs.shape[0]
    share = theta.shape[0]
    own = roots[0].shape[1]
    columns = poles.shape[1]
    me = lax.axis_index("row")
    cols = order.shape[1] // share
    target = lax.rem(lax.axis_index("col") + shift, cols)
    start = pl.multiple_of(target * share, LANES)
    for b in range(share // LANES):
        picks = column_of(order[:, pl.ds(pl.multiple_of(start + b * LANES, LANES), LANES)])
        total = jnp.zeros((LANES, own), F32)
        for s in range(count):
            base = partner(me, s, count) * own
            lane = lax.broadcasted_iota(I32, (LANES, own), 1) + base
            total = total + jnp.where(picks == lane, roots[s][...], 0.0)
        theta[b * LANES : (b + 1) * LANES, :] = jnp.broadcast_to(
            jnp.sum(total, axis=1, keepdims=True), (LANES, LANES)
        )

    tiles = panel.shape[1]
    block = tiles * LANES
    middle = columns // 2

    def make(slot, offset):
        for j in range(tiles):
            at = pl.ds(pl.multiple_of(offset + j * LANES, LANES), LANES)
            panel[slot, j] = (scaled[:, at] * (1.0 / (poles[:, at] - theta[...]))).astype(BF16)

    def dot(slot, offset):
        left = jnp.concatenate([panel[slot, j] for j in range(tiles)], axis=1)
        right = vecs[:, pl.ds(pl.multiple_of(offset, block), block)]
        return lax.dot_general(left, right, (((1,), (1,)), ((), ())), preferred_element_type=F32)

    def run(start, pairs):
        def body(i, carry):
            offset = start + i * (2 * block)
            make(1, offset + block)
            acc[...] += dot(0, offset)
            make(0, offset + 2 * block)
            acc[...] += dot(1, offset + block)
            return carry

        lax.fori_loop(0, pairs, body, 0)

    make(0, 0)
    acc[...] = jnp.zeros_like(acc)
    pairs = middle // (2 * block)
    if loads:
        run(0, pairs)
        for copy in copies:
            copy.wait()
        run(middle, pairs - 1)
    else:
        run(0, 2 * pairs - 1)
    make(1, columns - block)
    acc[...] += dot(0, columns - 2 * block)
    total = acc[...] + dot(1, columns - block)
    if shift == 0:
        out[...] = total
        return
    out[:nrows, :] = total.astype(BF16).T
    out[nrows:, :] = tail_rows(sums[:, pl.ds(start, share)], share)


def add_kernel(groups, product, sums, *refs):
    received, outs, full = refs[:-4], refs[-4:-1], refs[-1]
    share, nrows = product.shape
    norms = sums[:, pl.ds(pl.multiple_of(lax.axis_index("col") * share, LANES), share)]
    full[...] = product[...].T
    for ref in received:
        full[...] += ref[:nrows, :].astype(F32)
        norms = norms + ref[nrows : nrows + 1, :].astype(F32) + ref[nrows + 1 : nrows + 2, :].astype(F32)
    mine, other, total_norms = outs
    depth = nrows // groups
    half = lax.axis_index("half")
    for r in range(groups // 2):
        for which, ref in ((half, mine), (1 - half, other)):
            rows = pl.ds(pl.multiple_of((2 * r + which) * depth, depth), depth)
            ref[r * depth : (r + 1) * depth, :] = full[rows, :].astype(BF16)
    other[(groups // 2) * depth :, :] = tail_rows(norms, share)
    total_norms[...] = norms


def tail_rows(norms, share):
    high, low = split(norms)
    return jnp.concatenate([high, low, jnp.zeros((TAIL - 2, share), BF16)], axis=0)


def partner(index, step, size):
    if size & (size - 1) == 0:
        return index ^ step
    return lax.rem(index + size - step, size)


def exchange(value, axis, step):
    size = lax.axis_size(axis)
    pairs = [
        ((i ^ step) if size & (size - 1) == 0 else (i + size - step) % size, i) for i in range(size)
    ]
    return lax.ppermute(value, axis, pairs)


def message_kernel(count, depth, mine, got, norms, *outs):
    half = lax.axis_index("half")
    me = lax.axis_index("row")
    rows = count * depth
    share = mine.shape[1]
    total = norms[...] + got[rows : rows + 1, :].astype(F32) + got[rows + 1 : rows + 2, :].astype(F32)
    outs[-1][...] = total
    for s in range(count):
        at = pl.ds(pl.multiple_of(destination(me, s, count) * depth, depth), depth)
        first, second = mine[at, :], got[at, :]
        swap = half == 1
        out = outs[count - 1 - s]
        out[:depth, :] = jnp.where(swap, second, first)
        out[depth : 2 * depth, :] = jnp.where(swap, first, second)
        if s:
            out[2 * depth :, :] = tail_rows(total, share)


def destination(index, step, size):
    if size & (size - 1) == 0:
        return index ^ step
    return lax.rem(index + step, size)


def scale_kernel(count, depth, *refs):
    pieces, norms, out = refs[:count][::-1], refs[count], refs[count + 1]
    me = lax.axis_index("row")
    total = norms[...]
    for s in range(1, count):
        total = total + pieces[s][2 * depth : 2 * depth + 1, :].astype(F32)
        total = total + pieces[s][2 * depth + 1 : 2 * depth + 2, :].astype(F32)
    scale = lax.rsqrt(total + 1e-06)
    for s in range(count):
        value = (pieces[s][: 2 * depth, :].astype(F32) * scale).astype(BF16)
        out[partner(me, s, count)] = value


def body(vecs, poles, weights, kept, roots, order):
    row_count, col_count, halves = (lax.axis_size(a) for a in ("row", "col", "half"))
    own = roots.shape[0]
    width = order.shape[0]
    columns = poles.shape[1]
    nrows = vecs.shape[1]
    share = width // col_count
    groups = row_count * halves
    depth = nrows // groups
    direct = halves == 2 and depth % 16 == 0

    roots = roots.reshape(1, own)
    order = order.reshape(1, width)
    pieces = [roots] + [exchange(roots, "row", s) for s in range(1, row_count)]
    hbm = pl.BlockSpec(memory_space=pltpu.HBM)
    kept_bytes = 2 * nrows * columns + 4 * (2 * columns + own * row_count + 2 * width) + SLACK
    poles, roots_in, order, partial, scaled, sums = pl.pallas_call(
        norm_kernel,
        out_shape=(
            pltpu.VMEM((1, columns), F32),
            pltpu.VMEM((1, own), F32),
            pltpu.VMEM((1, width), I32),
            pltpu.VMEM((nrows, columns), BF16),
            pltpu.VMEM((1, columns), F32),
            pltpu.VMEM((1, width), F32),
        ),
        in_specs=[hbm] * 6,
        out_specs=(VMEM,) * 6,
        scratch_shapes=[
            pltpu.VMEM((1, columns), F32),
            pltpu.VMEM((1, columns), I32),
            pltpu.VMEM((own, LANES), F32),
            pltpu.SemaphoreType.DMA((5,)),
            pltpu.SemaphoreType.DMA((4,)),
        ],
        compiler_params=pltpu.CompilerParams(vmem_limit_bytes=VMEM_BYTES - kept_bytes),
        cost_estimate=pl.CostEstimate(
            flops=6 * own * columns, transcendentals=own * columns, bytes_accessed=nrows * columns
        ),
        name="norms",
    )(poles, weights, kept, roots, order, vecs)
    pieces[0] = roots_in
    block = tile_of(columns // 4, 2048)

    def panel(shift, loaded):
        loads = loaded is None
        args = (*pieces, order, poles, scaled, sums) + ((partial, vecs) if loads else (loaded,))
        out = pltpu.VMEM((nrows + TAIL, share), BF16) if shift else pltpu.VMEM((share, nrows), F32)
        results = pl.pallas_call(
            functools.partial(panel_kernel, row_count, shift, loads),
            out_shape=(out, pltpu.VMEM((nrows, columns), BF16)) if loads else (out,),
            in_specs=[VMEM] * (len(args) - 1) + [hbm if loads else VMEM],
            out_specs=(VMEM, VMEM) if loads else (VMEM,),
            input_output_aliases={len(args) - 2: 1} if loads else {},
            scratch_shapes=[
                pltpu.VMEM((share, LANES), F32),
                pltpu.VMEM((2, block // LANES, share, LANES), BF16),
                pltpu.VMEM((share, nrows), F32),
            ]
            + ([pltpu.SemaphoreType.DMA((4,))] if loads else []),
            compiler_params=pltpu.CompilerParams(
                vmem_limit_bytes=VMEM_BYTES - kept_bytes - 3 * nrows * columns if loads else 16 << 20
            ),
            cost_estimate=pl.CostEstimate(
                flops=2 * share * nrows * columns,
                transcendentals=share * columns,
                bytes_accessed=nrows * columns * 2,
            ),
            name=f"panel_{shift}",
        )(*args)
        return results if loads else (results[0], loaded)

    received = []
    loaded = None
    for shift in range(1, col_count):
        pairs = [(i, (i + shift) % col_count) for i in range(col_count)]
        message, loaded = panel(shift, loaded)
        received.append(lax.ppermute(message, "col", pairs))
    product, _ = panel(0, loaded)
    if not direct:
        full = jnp.transpose(product)
        norms = lax.dynamic_slice_in_dim(sums, lax.axis_index("col") * share, share, 1)
        for message in received:
            full = full + message[:nrows].astype(F32)
            norms = norms + jnp.sum(message[nrows : nrows + 2].astype(F32), axis=0, keepdims=True)
        norms = lax.psum(norms, ("row", "half"))
        moved = lax.all_to_all(
            full.astype(BF16).reshape(groups, depth, share),
            ("row", "half"),
            split_axis=0,
            concat_axis=0,
            tiled=True,
        )
        out = (moved.astype(F32) * lax.rsqrt(norms + 1e-06)).astype(BF16)
        return out.reshape(1, row_count, halves, depth, share)

    mine, other, norms = pl.pallas_call(
        functools.partial(add_kernel, groups),
        out_shape=(
            pltpu.VMEM((nrows // 2, share), BF16),
            pltpu.VMEM((nrows // 2 + TAIL, share), BF16),
            pltpu.VMEM((1, share), F32),
        ),
        in_specs=[VMEM] * (2 + len(received)),
        out_specs=(VMEM,) * 3,
        scratch_shapes=[pltpu.VMEM((nrows, share), F32)],
        compiler_params=params(4),
        name="add",
    )(product, sums, *received)
    got = exchange(other, "half", 1)
    shapes = [pltpu.VMEM((2 * depth + (TAIL if s else 0), share), BF16) for s in range(row_count - 1, -1, -1)]
    *messages, norms = pl.pallas_call(
        functools.partial(message_kernel, row_count, depth),
        out_shape=(*shapes, pltpu.VMEM((1, share), F32)),
        in_specs=[VMEM] * 3,
        out_specs=(VMEM,) * (row_count + 1),
        compiler_params=params(4),
        name="messages",
    )(mine, got, norms)
    landed = []
    for s in range(row_count - 1, 0, -1):
        pairs = [(i, destination_of(i, s, row_count)) for i in range(row_count)]
        landed.append(lax.ppermute(messages[row_count - 1 - s], "row", pairs))
    landed.append(messages[-1])
    out = pl.pallas_call(
        functools.partial(scale_kernel, row_count, depth),
        out_shape=jax.ShapeDtypeStruct((row_count, 2 * depth, share), BF16),
        in_specs=[VMEM] * (row_count + 1),
        out_specs=VMEM,
        compiler_params=params(4),
        name="scale",
    )(*landed, norms)
    return out.reshape(1, row_count, halves, depth, share)


def destination_of(index, step, size):
    return (index ^ step) if size & (size - 1) == 0 else (index + step) % size


def solution(mesh):
    return jax.shard_map(
        body,
        mesh=mesh,
        in_specs=(
            P(("grp", "half"), "row", "col"),
            P(("grp", "half"), "col"),
            P(("grp", "half"), "col"),
            P(("grp", "half"), "col"),
            P(("grp", "row")),
            P("grp"),
        ),
        out_specs=P(("grp", "row", "half"), None, None, None, "col"),
        check_vma=False,
    )
```

```python
import functools

import jax
import jax.numpy as jnp
from jax import lax
from jax.experimental import pallas as pl
from jax.experimental.pallas import tpu as pltpu
from jax.sharding import PartitionSpec as P

F32, BF16, I32 = jnp.float32, jnp.bfloat16, jnp.int32
LANES = 128
VMEM_BYTES = 67_043_328
SLACK = 32 << 10
MXU = 256
TAIL = 8
VMEM = pl.BlockSpec(memory_space=pltpu.VMEM)


def params(mib):
    return pltpu.CompilerParams(vmem_limit_bytes=mib << 20)


def tile_of(size, most):
    tile = most
    while size % tile:
        tile //= 2
    return tile


def column_of(row):
    n = row.shape[1]
    sub = lax.broadcasted_iota(I32, (n, n), 0)
    lane = lax.broadcasted_iota(I32, (n, n), 1)
    return jnp.sum(jnp.where(sub == lane, row, jnp.zeros_like(row)), axis=1, keepdims=True)


def split(value):
    high = value.astype(BF16)
    return high, (value - high.astype(F32)).astype(BF16)


def half_of(which, source, target, sem):
    parts = sem.shape[0]
    size = target.shape[1] // (2 * parts)
    spans = [slice((which * parts + i) * size, (which * parts + i + 1) * size) for i in range(parts)]
    return [
        pltpu.make_async_copy(source.at[0, :, at], target.at[:, at], sem.at[i]) for i, at in enumerate(spans)
    ]


def norm_kernel(poles, weights, kept, roots, order, vecs, *refs):
    poles_in, roots_in, order_in, vecs_in, scaled, sums = refs[:6]
    weights_in, kept_in, acc, sem, bulk = refs[6:]
    pairs = ((poles, poles_in), (weights, weights_in), (kept, kept_in), (roots, roots_in), (order, order_in))
    small = [pltpu.make_async_copy(a, b, sem.at[i]) for i, (a, b) in enumerate(pairs)]
    for copy in small:
        copy.start()
    columns = poles.shape[1]
    large = half_of(0, vecs, vecs_in, bulk)
    for copy in large:
        copy.start()
    for copy in small:
        copy.wait()
    own = roots.shape[1]
    theta = jnp.broadcast_to(column_of(roots_in[...]), (own, LANES))
    acc[...] = jnp.zeros_like(acc)
    step = tile_of(columns, 16 * LANES)

    def body(i, carry):
        total = acc[...]
        for j in range(step // LANES):
            at = pl.ds(pl.multiple_of(i * step + j * LANES, LANES), LANES)
            s = weights_in[:, at] * kept_in[:, at].astype(F32)
            scaled[:, at] = s
            c = s * (1.0 / (poles_in[:, at] - theta))
            total = total + c * c
        acc[...] = total
        return carry

    lax.fori_loop(0, columns // step, body, 0)
    column = jnp.sum(acc[...], axis=1, keepdims=True)
    base = lax.axis_index("row") * own
    sub = lax.broadcasted_iota(I32, (own, order.shape[1]), 0)
    hit = (order_in[...] - base) == sub
    sums[...] = jnp.sum(jnp.where(hit, column, 0.0), axis=0, keepdims=True)
    for copy in large:
        copy.wait()


def panel_kernel(chip, count, shift, loads, *refs):
    roots = refs[:count]
    if loads:
        order, poles, scaled, sums, _, source, out, vecs, theta, acc, sem = refs[count:]
        copies = half_of(1, source, vecs, sem)
        for copy in copies:
            copy.start()
    else:
        order, poles, scaled, sums, vecs, out, theta, acc = refs[count:]
        copies = []
    nrows = vecs.shape[0]
    share = theta.shape[0]
    own = roots[0].shape[1]
    columns = poles.shape[1]
    me = lax.axis_index("row")
    cols = order.shape[1] // share
    target = lax.rem(lax.axis_index("col") + shift, cols)
    start = pl.multiple_of(target * share, LANES)
    for b in range(share // LANES):
        picks = column_of(order[:, pl.ds(pl.multiple_of(start + b * LANES, LANES), LANES)])
        total = jnp.zeros((LANES, own), F32)
        for s in range(count):
            base = partner(me, s, count) * own
            lane = lax.broadcasted_iota(I32, (LANES, own), 1) + base
            total = total + jnp.where(picks == lane, roots[s][...], 0.0)
        theta[b * LANES : (b + 1) * LANES, :] = jnp.broadcast_to(
            jnp.sum(total, axis=1, keepdims=True), (LANES, LANES)
        )

    tile = MXU
    most = tile_of(columns // (2 * tile), 32)

    def run(start, trips, units):
        def body(i, carry):
            for t in range(most):
                offset = start + i * (most * tile) + t * tile
                at = [pl.ds(pl.multiple_of(offset + j * LANES, LANES), LANES) for j in range(tile // LANES)]
                panel = [(scaled[:, c] * (1.0 / (poles[:, c] - theta[...]))).astype(BF16) for c in at]
                unit, register = t % 2, (t // 2) % 2
                right = vecs[:, pl.ds(pl.multiple_of(offset, tile), tile)]
                pltpu.matmul_push_rhs(right, staging_register=register, mxu_index=unit, transpose=True)
                pltpu.matmul_acc_lhs(units[unit], jnp.concatenate(panel, axis=1), load_staged_rhs=register)
            return carry

        lax.fori_loop(0, trips, body, 0)

    def multiply(*units):
        trips = columns // (2 * most * tile)
        if loads:
            run(0, trips, units)
            for copy in copies:
                copy.wait()
            run(columns // 2, trips, units)
        else:
            run(0, 2 * trips, units)
        acc[...] = pltpu.matmul_pop(units[0]) + pltpu.matmul_pop(units[1])

    with jax.sharding.use_abstract_mesh(chip):
        pl.run_scoped(multiply, *(pltpu.ACC(unit)((share, nrows), F32) for unit in range(2)))
    total = acc[...]
    if shift == 0:
        out[...] = total
        return
    out[:nrows, :] = total.astype(BF16).T
    out[nrows:, :] = tail_rows(sums[:, pl.ds(start, share)], share)


def add_kernel(groups, product, sums, *refs):
    received, outs, full = refs[:-4], refs[-4:-1], refs[-1]
    share, nrows = product.shape
    norms = sums[:, pl.ds(pl.multiple_of(lax.axis_index("col") * share, LANES), share)]
    full[...] = product[...].T
    for ref in received:
        full[...] += ref[:nrows, :].astype(F32)
        norms = norms + ref[nrows : nrows + 1, :].astype(F32) + ref[nrows + 1 : nrows + 2, :].astype(F32)
    mine, other, total_norms = outs
    depth = nrows // groups
    half = lax.axis_index("half")
    for r in range(groups // 2):
        for which, ref in ((half, mine), (1 - half, other)):
            rows = pl.ds(pl.multiple_of((2 * r + which) * depth, depth), depth)
            ref[r * depth : (r + 1) * depth, :] = full[rows, :].astype(BF16)
    other[(groups // 2) * depth :, :] = tail_rows(norms, share)
    total_norms[...] = norms


def tail_rows(norms, share):
    high, low = split(norms)
    return jnp.concatenate([high, low, jnp.zeros((TAIL - 2, share), BF16)], axis=0)


def partner(index, step, size):
    if size & (size - 1) == 0:
        return index ^ step
    return lax.rem(index + size - step, size)


def exchange(value, axis, step):
    size = lax.axis_size(axis)
    pairs = [
        ((i ^ step) if size & (size - 1) == 0 else (i + size - step) % size, i) for i in range(size)
    ]
    return lax.ppermute(value, axis, pairs)


def message_kernel(count, depth, mine, got, norms, *outs):
    half = lax.axis_index("half")
    me = lax.axis_index("row")
    rows = count * depth
    share = mine.shape[1]
    total = norms[...] + got[rows : rows + 1, :].astype(F32) + got[rows + 1 : rows + 2, :].astype(F32)
    outs[-1][...] = total
    for s in range(count):
        at = pl.ds(pl.multiple_of(destination(me, s, count) * depth, depth), depth)
        first, second = mine[at, :], got[at, :]
        swap = half == 1
        out = outs[count - 1 - s]
        out[:depth, :] = jnp.where(swap, second, first)
        out[depth : 2 * depth, :] = jnp.where(swap, first, second)
        if s:
            out[2 * depth :, :] = tail_rows(total, share)


def destination(index, step, size):
    if size & (size - 1) == 0:
        return index ^ step
    return lax.rem(index + step, size)


def scale_kernel(count, depth, *refs):
    pieces, norms, out = refs[:count][::-1], refs[count], refs[count + 1]
    me = lax.axis_index("row")
    total = norms[...]
    for s in range(1, count):
        total = total + pieces[s][2 * depth : 2 * depth + 1, :].astype(F32)
        total = total + pieces[s][2 * depth + 1 : 2 * depth + 2, :].astype(F32)
    scale = lax.rsqrt(total + 1e-06)
    for s in range(count):
        value = (pieces[s][: 2 * depth, :].astype(F32) * scale).astype(BF16)
        out[partner(me, s, count)] = value


def body(chip, vecs, poles, weights, kept, roots, order):
    row_count, col_count, halves = (lax.axis_size(a) for a in ("row", "col", "half"))
    own = roots.shape[0]
    width = order.shape[0]
    columns = poles.shape[1]
    nrows = vecs.shape[1]
    share = width // col_count
    groups = row_count * halves
    depth = nrows // groups
    direct = halves == 2 and depth % 16 == 0

    roots = roots.reshape(1, own)
    order = order.reshape(1, width)
    pieces = [roots] + [exchange(roots, "row", s) for s in range(1, row_count)]
    hbm = pl.BlockSpec(memory_space=pltpu.HBM)
    kept_bytes = 2 * nrows * columns + 4 * (2 * columns + own * row_count + 2 * width) + SLACK
    poles, roots_in, order, partial, scaled, sums = pl.pallas_call(
        norm_kernel,
        out_shape=(
            pltpu.VMEM((1, columns), F32),
            pltpu.VMEM((1, own), F32),
            pltpu.VMEM((1, width), I32),
            pltpu.VMEM((nrows, columns), BF16),
            pltpu.VMEM((1, columns), F32),
            pltpu.VMEM((1, width), F32),
        ),
        in_specs=[hbm] * 6,
        out_specs=(VMEM,) * 6,
        scratch_shapes=[
            pltpu.VMEM((1, columns), F32),
            pltpu.VMEM((1, columns), I32),
            pltpu.VMEM((own, LANES), F32),
            pltpu.SemaphoreType.DMA((5,)),
            pltpu.SemaphoreType.DMA((4,)),
        ],
        compiler_params=pltpu.CompilerParams(vmem_limit_bytes=VMEM_BYTES - kept_bytes),
        cost_estimate=pl.CostEstimate(
            flops=6 * own * columns, transcendentals=own * columns, bytes_accessed=nrows * columns
        ),
        name="norms",
    )(poles, weights, kept, roots, order, vecs)
    pieces[0] = roots_in
    def panel(shift, loaded):
        loads = loaded is None
        args = (*pieces, order, poles, scaled, sums) + ((partial, vecs) if loads else (loaded,))
        out = pltpu.VMEM((nrows + TAIL, share), BF16) if shift else pltpu.VMEM((share, nrows), F32)
        results = pl.pallas_call(
            functools.partial(panel_kernel, chip, row_count, shift, loads),
            out_shape=(out, pltpu.VMEM((nrows, columns), BF16)) if loads else (out,),
            in_specs=[VMEM] * (len(args) - 1) + [hbm if loads else VMEM],
            out_specs=(VMEM, VMEM) if loads else (VMEM,),
            input_output_aliases={len(args) - 2: 1} if loads else {},
            scratch_shapes=[
                pltpu.VMEM((share, LANES), F32),
                pltpu.VMEM((share, nrows), F32),
            ]
            + ([pltpu.SemaphoreType.DMA((4,))] if loads else []),
            compiler_params=pltpu.CompilerParams(
                vmem_limit_bytes=VMEM_BYTES - kept_bytes - 3 * nrows * columns if loads else 16 << 20
            ),
            cost_estimate=pl.CostEstimate(
                flops=2 * share * nrows * columns,
                transcendentals=share * columns,
                bytes_accessed=nrows * columns * 2,
            ),
            name=f"panel_{shift}",
        )(*args)
        return results if loads else (results[0], loaded)

    received = []
    loaded = None
    for shift in range(1, col_count):
        pairs = [(i, (i + shift) % col_count) for i in range(col_count)]
        message, loaded = panel(shift, loaded)
        received.append(lax.ppermute(message, "col", pairs))
    product, _ = panel(0, loaded)
    if not direct:
        full = jnp.transpose(product)
        norms = lax.dynamic_slice_in_dim(sums, lax.axis_index("col") * share, share, 1)
        for message in received:
            full = full + message[:nrows].astype(F32)
            norms = norms + jnp.sum(message[nrows : nrows + 2].astype(F32), axis=0, keepdims=True)
        norms = lax.psum(norms, ("row", "half"))
        moved = lax.all_to_all(
            full.astype(BF16).reshape(groups, depth, share),
            ("row", "half"),
            split_axis=0,
            concat_axis=0,
            tiled=True,
        )
        out = (moved.astype(F32) * lax.rsqrt(norms + 1e-06)).astype(BF16)
        return out.reshape(1, row_count, halves, depth, share)

    mine, other, norms = pl.pallas_call(
        functools.partial(add_kernel, groups),
        out_shape=(
            pltpu.VMEM((nrows // 2, share), BF16),
            pltpu.VMEM((nrows // 2 + TAIL, share), BF16),
            pltpu.VMEM((1, share), F32),
        ),
        in_specs=[VMEM] * (2 + len(received)),
        out_specs=(VMEM,) * 3,
        scratch_shapes=[pltpu.VMEM((nrows, share), F32)],
        compiler_params=params(4),
        name="add",
    )(product, sums, *received)
    got = exchange(other, "half", 1)
    shapes = [pltpu.VMEM((2 * depth + (TAIL if s else 0), share), BF16) for s in range(row_count - 1, -1, -1)]
    *messages, norms = pl.pallas_call(
        functools.partial(message_kernel, row_count, depth),
        out_shape=(*shapes, pltpu.VMEM((1, share), F32)),
        in_specs=[VMEM] * 3,
        out_specs=(VMEM,) * (row_count + 1),
        compiler_params=params(4),
        name="messages",
    )(mine, got, norms)
    landed = []
    for s in range(row_count - 1, 0, -1):
        pairs = [(i, destination_of(i, s, row_count)) for i in range(row_count)]
        landed.append(lax.ppermute(messages[row_count - 1 - s], "row", pairs))
    landed.append(messages[-1])
    out = pl.pallas_call(
        functools.partial(scale_kernel, row_count, depth),
        out_shape=jax.ShapeDtypeStruct((row_count, 2 * depth, share), BF16),
        in_specs=[VMEM] * (row_count + 1),
        out_specs=VMEM,
        compiler_params=params(4),
        name="scale",
    )(*landed, norms)
    return out.reshape(1, row_count, halves, depth, share)


def destination_of(index, step, size):
    return (index ^ step) if size & (size - 1) == 0 else (index + step) % size


def solution(mesh):
    return jax.shard_map(
        functools.partial(body, mesh.abstract_mesh),
        mesh=mesh,
        in_specs=(
            P(("grp", "half"), "row", "col"),
            P(("grp", "half"), "col"),
            P(("grp", "half"), "col"),
            P(("grp", "half"), "col"),
            P(("grp", "row")),
            P("grp"),
        ),
        out_specs=P(("grp", "row", "half"), None, None, None, "col"),
        check_vma=False,
    )
```

```python
import functools

import jax
import jax.numpy as jnp
from jax import lax
from jax.experimental import pallas as pl
from jax.experimental.pallas import tpu as pltpu
from jax.sharding import PartitionSpec as P

F32, BF16, I32 = jnp.float32, jnp.bfloat16, jnp.int32
LANES = 128
VMEM_BYTES = 67_043_328
SLACK = 32 << 10
MXU = 256
PARTS = ((0, 2), (2, 5), (5, 8))
TAIL = 8
VMEM = pl.BlockSpec(memory_space=pltpu.VMEM)


def params(mib):
    return pltpu.CompilerParams(vmem_limit_bytes=mib << 20)


def tile_of(size, most):
    tile = most
    while size % tile:
        tile //= 2
    return tile


def column_of(row):
    n = row.shape[1]
    sub = lax.broadcasted_iota(I32, (n, n), 0)
    lane = lax.broadcasted_iota(I32, (n, n), 1)
    return jnp.sum(jnp.where(sub == lane, row, jnp.zeros_like(row)), axis=1, keepdims=True)


def split(value):
    high = value.astype(BF16)
    return high, (value - high.astype(F32)).astype(BF16)


def part_of(source, target, span, sem):
    size = target.shape[1] // 8
    at = slice(span[0] * size, span[1] * size)
    return pltpu.make_async_copy(source.at[0, :, at], target.at[:, at], sem)


def squares(poles, scaled, theta, start, stop, total):
    step = tile_of(stop - start, 16 * LANES)

    def body(i, total):
        for j in range(step // LANES):
            at = pl.ds(pl.multiple_of(start + i * step + j * LANES, LANES), LANES)
            c = scaled[:, at] * (1.0 / (poles[:, at] - theta))
            total = total + c * c
        return total

    return lax.fori_loop(0, (stop - start) // step, body, total)


def first_kernel(poles, weights, kept, roots, order, vecs, *refs):
    poles_in, roots_in, order_in, vecs_in, scaled, squared = refs[:6]
    weights_in, kept_in, sem, bulk = refs[6:]
    pairs = ((poles, poles_in), (weights, weights_in), (kept, kept_in), (roots, roots_in), (order, order_in))
    small = [pltpu.make_async_copy(a, b, sem.at[i]) for i, (a, b) in enumerate(pairs)]
    for copy in small:
        copy.start()
    large = part_of(vecs, vecs_in, PARTS[0], bulk)
    large.start()
    for copy in small:
        copy.wait()
    own = roots.shape[1]
    columns = poles.shape[1]
    scaled[...] = weights_in[...] * kept_in[...].astype(F32)
    theta = jnp.broadcast_to(column_of(roots_in[...]), (own, LANES))
    squared[...] = squares(poles_in, scaled, theta, 0, columns // 2, jnp.zeros((own, LANES), F32))
    large.wait()


def second_kernel(poles, scaled, squared, roots, order, _, vecs, vecs_in, sums, bulk):
    large = part_of(vecs, vecs_in, PARTS[1], bulk)
    large.start()
    own = roots.shape[1]
    columns = poles.shape[1]
    theta = jnp.broadcast_to(column_of(roots[...]), (own, LANES))
    total = squares(poles, scaled, theta, columns // 2, columns, squared[...])
    column = jnp.sum(total, axis=1, keepdims=True)
    base = lax.axis_index("row") * own
    sub = lax.broadcasted_iota(I32, (own, order.shape[1]), 0)
    hit = (order[...] - base) == sub
    sums[...] = jnp.sum(jnp.where(hit, column, 0.0), axis=0, keepdims=True)
    large.wait()


def panel_kernel(chip, doubling, count, shift, loads, *refs):
    roots = refs[:count]
    if loads:
        order, poles, scaled, sums, _, source, out, vecs, theta, acc, sem = refs[count:]
        copy = part_of(source, vecs, PARTS[2], sem)
        copy.start()
    else:
        order, poles, scaled, sums, vecs, out, theta, acc = refs[count:]
    nrows = vecs.shape[0]
    share = theta.shape[0]
    own = roots[0].shape[1]
    columns = poles.shape[1]
    me = lax.axis_index("row")
    cols = order.shape[1] // share
    target = lax.rem(lax.axis_index("col") + shift, cols)
    start = pl.multiple_of(target * share, LANES)
    for b in range(share // LANES):
        picks = column_of(order[:, pl.ds(pl.multiple_of(start + b * LANES, LANES), LANES)])
        total = jnp.zeros((LANES, 1), F32)
        for s in range(count):
            lane = lax.broadcasted_iota(I32, (LANES, roots[s].shape[1]), 1)
            if doubling:
                first = (1 << s) >> 1
                lane = ((lane // own + first) ^ me) * own + lane % own
            else:
                lane = lane + partner(me, s, count) * own
            total = total + jnp.sum(jnp.where(picks == lane, roots[s][...], 0.0), axis=1, keepdims=True)
        theta[b * LANES : (b + 1) * LANES, :] = jnp.broadcast_to(total, (LANES, LANES))

    tile = MXU

    def run(start, stop, units):
        for t in range(start // tile, stop // tile):
            at = [slice(t * tile + j * LANES, t * tile + (j + 1) * LANES) for j in range(tile // LANES)]
            panel = [(scaled[:, c] * (1.0 / (poles[:, c] - theta[...]))).astype(BF16) for c in at]
            unit, register = t % 2, (t // 2) % 2
            right = vecs[:, t * tile : (t + 1) * tile]
            pltpu.matmul_push_rhs(right, staging_register=register, mxu_index=unit, transpose=True)
            pltpu.matmul_acc_lhs(units[unit], jnp.concatenate(panel, axis=1), load_staged_rhs=register)

    def multiply(*units):
        here = PARTS[2][0] * (columns // 8) if loads else columns
        run(0, here, units)
        if loads:
            copy.wait()
            run(here, columns, units)
        acc[...] = pltpu.matmul_pop(units[0]) + pltpu.matmul_pop(units[1])

    with jax.sharding.use_abstract_mesh(chip):
        pl.run_scoped(multiply, *(pltpu.ACC(unit)((share, nrows), F32) for unit in range(2)))
    total = acc[...]
    if shift == 0:
        out[...] = total
        return
    out[:nrows, :] = total.astype(BF16).T
    out[nrows:, :] = tail_rows(sums[:, pl.ds(start, share)], share)


def add_kernel(groups, product, sums, *refs):
    received, outs, full = refs[:-4], refs[-4:-1], refs[-1]
    share, nrows = product.shape
    norms = sums[:, pl.ds(pl.multiple_of(lax.axis_index("col") * share, LANES), share)]
    full[...] = product[...].T
    for ref in received:
        full[...] += ref[:nrows, :].astype(F32)
        norms = norms + ref[nrows : nrows + 1, :].astype(F32) + ref[nrows + 1 : nrows + 2, :].astype(F32)
    mine, other, total_norms = outs
    depth = nrows // groups
    half = lax.axis_index("half")
    for r in range(groups // 2):
        for which, ref in ((half, mine), (1 - half, other)):
            rows = pl.ds(pl.multiple_of((2 * r + which) * depth, depth), depth)
            ref[r * depth : (r + 1) * depth, :] = full[rows, :].astype(BF16)
    other[(groups // 2) * depth :, :] = tail_rows(norms, share)
    total_norms[...] = norms


def tail_rows(norms, share):
    high, low = split(norms)
    return jnp.concatenate([high, low, jnp.zeros((TAIL - 2, share), BF16)], axis=0)


def partner(index, step, size):
    if size & (size - 1) == 0:
        return index ^ step
    return lax.rem(index + size - step, size)


def exchange(value, axis, step):
    size = lax.axis_size(axis)
    pairs = [
        ((i ^ step) if size & (size - 1) == 0 else (i + size - step) % size, i) for i in range(size)
    ]
    return lax.ppermute(value, axis, pairs)


def message_kernel(count, depth, mine, got, norms, *outs):
    half = lax.axis_index("half")
    me = lax.axis_index("row")
    rows = count * depth
    share = mine.shape[1]
    total = norms[...] + got[rows : rows + 1, :].astype(F32) + got[rows + 1 : rows + 2, :].astype(F32)
    outs[-1][...] = total
    for s in range(count):
        at = pl.ds(pl.multiple_of(destination(me, s, count) * depth, depth), depth)
        first, second = mine[at, :], got[at, :]
        swap = half == 1
        out = outs[count - 1 - s]
        out[:depth, :] = jnp.where(swap, second, first)
        out[depth : 2 * depth, :] = jnp.where(swap, first, second)
        if s:
            out[2 * depth :, :] = tail_rows(total, share)


def destination(index, step, size):
    if size & (size - 1) == 0:
        return index ^ step
    return lax.rem(index + step, size)


def scale_kernel(count, depth, *refs):
    pieces, norms, out = refs[:count][::-1], refs[count], refs[count + 1]
    me = lax.axis_index("row")
    total = norms[...]
    for s in range(1, count):
        total = total + pieces[s][2 * depth : 2 * depth + 1, :].astype(F32)
        total = total + pieces[s][2 * depth + 1 : 2 * depth + 2, :].astype(F32)
    scale = lax.rsqrt(total + 1e-06)
    for s in range(count):
        value = (pieces[s][: 2 * depth, :].astype(F32) * scale).astype(BF16)
        out[partner(me, s, count)] = value


def body(chip, vecs, poles, weights, kept, roots, order):
    row_count, col_count, halves = (lax.axis_size(a) for a in ("row", "col", "half"))
    own = roots.shape[0]
    width = order.shape[0]
    columns = poles.shape[1]
    nrows = vecs.shape[1]
    share = width // col_count
    groups = row_count * halves
    depth = nrows // groups
    direct = halves == 2 and depth % 16 == 0

    roots = roots.reshape(1, own)
    order = order.reshape(1, width)
    hbm = pl.BlockSpec(memory_space=pltpu.HBM)
    kept_bytes = 2 * nrows * columns + 4 * (2 * columns + own * (row_count + LANES + 1) + 2 * width) + SLACK
    loading = pltpu.CompilerParams(vmem_limit_bytes=VMEM_BYTES - kept_bytes - 3 * nrows * columns)
    poles, roots_in, order, started, scaled, squared = pl.pallas_call(
        first_kernel,
        out_shape=(
            pltpu.VMEM((1, columns), F32),
            pltpu.VMEM((1, own), F32),
            pltpu.VMEM((1, width), I32),
            pltpu.VMEM((nrows, columns), BF16),
            pltpu.VMEM((1, columns), F32),
            pltpu.VMEM((own, LANES), F32),
        ),
        in_specs=[hbm] * 6,
        out_specs=(VMEM,) * 6,
        scratch_shapes=[
            pltpu.VMEM((1, columns), F32),
            pltpu.VMEM((1, columns), I32),
            pltpu.SemaphoreType.DMA((5,)),
            pltpu.SemaphoreType.DMA,
        ],
        compiler_params=pltpu.CompilerParams(vmem_limit_bytes=VMEM_BYTES - kept_bytes),
        cost_estimate=pl.CostEstimate(
            flops=3 * own * columns, transcendentals=own * columns // 2, bytes_accessed=nrows * columns
        ),
        name="norms_first",
    )(poles, weights, kept, roots, order, vecs)
    doubling = row_count & (row_count - 1) == 0 and own & (own - 1) == 0
    if doubling:
        pieces = [roots]
        step = 1
        while step < row_count:
            if step == 2:
                last, squared = lax.optimization_barrier((pieces.pop(), squared))
                pieces = [roots_in, last]
            pieces.append(exchange(jnp.concatenate(pieces, axis=1), "row", step))
            step *= 2
    else:
        pieces = [roots] + [exchange(roots, "row", s) for s in range(1, row_count)]
    pieces[0] = roots_in
    started, sums = pl.pallas_call(
        second_kernel,
        out_shape=(pltpu.VMEM((nrows, columns), BF16), pltpu.VMEM((1, width), F32)),
        in_specs=[VMEM] * 6 + [hbm],
        out_specs=(VMEM, VMEM),
        input_output_aliases={5: 0},
        scratch_shapes=[pltpu.SemaphoreType.DMA],
        compiler_params=loading,
        cost_estimate=pl.CostEstimate(
            flops=3 * own * columns, transcendentals=own * columns // 2, bytes_accessed=nrows * columns
        ),
        name="norms_second",
    )(poles, scaled, squared, roots_in, order, started, vecs)

    def panel(shift, loaded):
        loads = loaded is None
        args = (*pieces, order, poles, scaled, sums) + ((started, vecs) if loads else (loaded,))
        out = pltpu.VMEM((nrows + TAIL, share), BF16) if shift else pltpu.VMEM((share, nrows), F32)
        results = pl.pallas_call(
            functools.partial(panel_kernel, chip, doubling, len(pieces), shift, loads),
            out_shape=(out, pltpu.VMEM((nrows, columns), BF16)) if loads else (out,),
            in_specs=[VMEM] * (len(args) - 1) + [hbm if loads else VMEM],
            out_specs=(VMEM, VMEM) if loads else (VMEM,),
            input_output_aliases={len(args) - 2: 1} if loads else {},
            scratch_shapes=[
                pltpu.VMEM((share, LANES), F32),
                pltpu.VMEM((share, nrows), F32),
            ]
            + ([pltpu.SemaphoreType.DMA] if loads else []),
            compiler_params=loading if loads else params(16),
            cost_estimate=pl.CostEstimate(
                flops=2 * share * nrows * columns,
                transcendentals=share * columns,
                bytes_accessed=nrows * columns * 2,
            ),
            name=f"panel_{shift}",
        )(*args)
        return results if loads else (results[0], loaded)

    received = []
    loaded = None
    for shift in range(1, col_count):
        pairs = [(i, (i + shift) % col_count) for i in range(col_count)]
        message, loaded = panel(shift, loaded)
        received.append(lax.ppermute(message, "col", pairs))
    product, _ = panel(0, loaded)
    if not direct:
        full = jnp.transpose(product)
        norms = lax.dynamic_slice_in_dim(sums, lax.axis_index("col") * share, share, 1)
        for message in received:
            full = full + message[:nrows].astype(F32)
            norms = norms + jnp.sum(message[nrows : nrows + 2].astype(F32), axis=0, keepdims=True)
        norms = lax.psum(norms, ("row", "half"))
        moved = lax.all_to_all(
            full.astype(BF16).reshape(groups, depth, share),
            ("row", "half"),
            split_axis=0,
            concat_axis=0,
            tiled=True,
        )
        out = (moved.astype(F32) * lax.rsqrt(norms + 1e-06)).astype(BF16)
        return out.reshape(1, row_count, halves, depth, share)

    mine, other, norms = pl.pallas_call(
        functools.partial(add_kernel, groups),
        out_shape=(
            pltpu.VMEM((nrows // 2, share), BF16),
            pltpu.VMEM((nrows // 2 + TAIL, share), BF16),
            pltpu.VMEM((1, share), F32),
        ),
        in_specs=[VMEM] * (2 + len(received)),
        out_specs=(VMEM,) * 3,
        scratch_shapes=[pltpu.VMEM((nrows, share), F32)],
        compiler_params=params(4),
        name="add",
    )(product, sums, *received)
    got = exchange(other, "half", 1)
    shapes = [pltpu.VMEM((2 * depth + (TAIL if s else 0), share), BF16) for s in range(row_count - 1, -1, -1)]
    *messages, norms = pl.pallas_call(
        functools.partial(message_kernel, row_count, depth),
        out_shape=(*shapes, pltpu.VMEM((1, share), F32)),
        in_specs=[VMEM] * 3,
        out_specs=(VMEM,) * (row_count + 1),
        compiler_params=params(4),
        name="messages",
    )(mine, got, norms)
    landed = []
    for s in range(row_count - 1, 0, -1):
        pairs = [(i, destination_of(i, s, row_count)) for i in range(row_count)]
        landed.append(lax.ppermute(messages[row_count - 1 - s], "row", pairs))
    landed.append(messages[-1])
    out = pl.pallas_call(
        functools.partial(scale_kernel, row_count, depth),
        out_shape=jax.ShapeDtypeStruct((row_count, 2 * depth, share), BF16),
        in_specs=[VMEM] * (row_count + 1),
        out_specs=VMEM,
        compiler_params=params(4),
        name="scale",
    )(*landed, norms)
    return out.reshape(1, row_count, halves, depth, share)


def destination_of(index, step, size):
    return (index ^ step) if size & (size - 1) == 0 else (index + step) % size


def solution(mesh):
    return jax.shard_map(
        functools.partial(body, mesh.abstract_mesh),
        mesh=mesh,
        in_specs=(
            P(("grp", "half"), "row", "col"),
            P(("grp", "half"), "col"),
            P(("grp", "half"), "col"),
            P(("grp", "half"), "col"),
            P(("grp", "row")),
            P("grp"),
        ),
        out_specs=P(("grp", "row", "half"), None, None, None, "col"),
        check_vma=False,
    )
```

```python
import functools

import jax
import jax.numpy as jnp
from jax import lax
from jax.experimental import pallas as pl
from jax.experimental.pallas import tpu as pltpu
from jax.sharding import PartitionSpec as P

F32, BF16, I32 = jnp.float32, jnp.bfloat16, jnp.int32
LANES = 128
VMEM_BYTES = 67_043_328
SLACK = 32 << 10
MXU = 256
PARTS = ((0, 6), (6, 8))
TAIL = 8
VMEM = pl.BlockSpec(memory_space=pltpu.VMEM)


def params(mib):
    return pltpu.CompilerParams(vmem_limit_bytes=mib << 20)


def tile_of(size, most):
    tile = most
    while size % tile:
        tile //= 2
    return tile


def column_of(row):
    n = row.shape[1]
    sub = lax.broadcasted_iota(I32, (n, n), 0)
    lane = lax.broadcasted_iota(I32, (n, n), 1)
    return jnp.sum(jnp.where(sub == lane, row, jnp.zeros_like(row)), axis=1, keepdims=True)


def split(value):
    high = value.astype(BF16)
    return high, (value - high.astype(F32)).astype(BF16)


def part_of(source, target, span, sem):
    size = target.shape[1] // 8
    at = slice(span[0] * size, span[1] * size)
    return pltpu.make_async_copy(source.at[0, :, at], target.at[:, at], sem)


def squares(poles, scaled, theta):
    columns = poles.shape[1]
    step = tile_of(columns, 16 * LANES)

    def body(i, total):
        for j in range(step // LANES):
            at = pl.ds(pl.multiple_of(i * step + j * LANES, LANES), LANES)
            c = scaled[:, at] * (1.0 / (poles[:, at] - theta))
            total = total + c * c
        return total

    return lax.fori_loop(0, columns // step, body, jnp.zeros(theta.shape, F32))


def norm_kernel(poles, weights, kept, roots, order, vecs, *refs):
    poles_in, roots_in, order_in, vecs_in, scaled, sums = refs[:6]
    weights_in, kept_in, sem, bulk = refs[6:]
    pairs = ((poles, poles_in), (weights, weights_in), (kept, kept_in), (roots, roots_in), (order, order_in))
    small = [pltpu.make_async_copy(a, b, sem.at[i]) for i, (a, b) in enumerate(pairs)]
    for copy in small:
        copy.start()
    large = part_of(vecs, vecs_in, PARTS[0], bulk)
    large.start()
    for copy in small:
        copy.wait()
    own = roots.shape[1]
    scaled[...] = weights_in[...] * kept_in[...].astype(F32)
    theta = jnp.broadcast_to(column_of(roots_in[...]), (own, LANES))
    total = squares(poles_in, scaled, theta)
    column = jnp.sum(total, axis=1, keepdims=True)
    base = lax.axis_index("row") * own
    sub = lax.broadcasted_iota(I32, (own, order.shape[1]), 0)
    hit = (order_in[...] - base) == sub
    sums[...] = jnp.sum(jnp.where(hit, column, 0.0), axis=0, keepdims=True)
    large.wait()


def panel_kernel(chip, count, shift, loads, *refs):
    roots = refs[:count]
    if loads:
        order, poles, scaled, sums, _, source, out, vecs, theta, acc, sem = refs[count:]
        copy = part_of(source, vecs, PARTS[1], sem)
        copy.start()
    else:
        order, poles, scaled, sums, vecs, out, theta, acc = refs[count:]
    nrows = vecs.shape[0]
    share = theta.shape[0]
    own = roots[0].shape[1]
    columns = poles.shape[1]
    me = lax.axis_index("row")
    cols = lax.axis_size("col")
    target = lax.rem(lax.axis_index("col") + shift, cols)
    start = pl.multiple_of(target * share, LANES)
    for b in range(share // LANES):
        picks = column_of(order[:, pl.ds(pl.multiple_of(start + b * LANES, LANES), LANES)])
        total = jnp.zeros((LANES, 1), F32)
        for s in range(count):
            lane = lax.broadcasted_iota(I32, (LANES, roots[s].shape[1]), 1)
            lane = lane + partner(me, s, count) * own
            total = total + jnp.sum(jnp.where(picks == lane, roots[s][...], 0.0), axis=1, keepdims=True)
        theta[b * LANES : (b + 1) * LANES, :] = jnp.broadcast_to(total, (LANES, LANES))

    tile = MXU

    def run(start, stop, units):
        for t in range(start // tile, stop // tile):
            at = [slice(t * tile + j * LANES, t * tile + (j + 1) * LANES) for j in range(tile // LANES)]
            panel = [(scaled[:, c] * (1.0 / (poles[:, c] - theta[...]))).astype(BF16) for c in at]
            unit, register = t % 2, (t // 2) % 2
            right = vecs[:, t * tile : (t + 1) * tile]
            pltpu.matmul_push_rhs(right, staging_register=register, mxu_index=unit, transpose=True)
            pltpu.matmul_acc_lhs(units[unit], jnp.concatenate(panel, axis=1), load_staged_rhs=register)

    def multiply(*units):
        here = PARTS[1][0] * (columns // 8) if loads else columns
        run(0, here, units)
        if loads:
            copy.wait()
            run(here, columns, units)
        acc[...] = pltpu.matmul_pop(units[0]) + pltpu.matmul_pop(units[1])

    with jax.sharding.use_abstract_mesh(chip):
        pl.run_scoped(multiply, *(pltpu.ACC(unit)((share, nrows), F32) for unit in range(2)))
    total = acc[...]
    if shift == 0:
        out[...] = total
        return
    out[:nrows, :] = total.astype(BF16).T
    out[nrows:, :] = tail_rows(sums[:, pl.ds(start, share)], share)


def add_kernel(groups, product, sums, *refs):
    received, outs, full = refs[:-4], refs[-4:-1], refs[-1]
    share, nrows = product.shape
    full[...] = product[...].T
    total_norms = outs[2]
    total_norms[...] = sums[:, pl.ds(pl.multiple_of(lax.axis_index("col") * share, LANES), share)]
    for ref in received:
        full[...] += ref[:nrows, :].astype(F32)
        total_norms[...] += ref[nrows : nrows + 1, :].astype(F32) + ref[nrows + 1 : nrows + 2, :].astype(F32)
    norms = total_norms[...]
    mine, other = outs[:2]
    depth = nrows // groups
    half = lax.axis_index("half")
    for r in range(groups // 2):
        for which, ref in ((half, mine), (1 - half, other)):
            rows = pl.ds(pl.multiple_of((2 * r + which) * depth, depth), depth)
            ref[r * depth : (r + 1) * depth, :] = full[rows, :].astype(BF16)
    other[(groups // 2) * depth :, :] = tail_rows(norms, share)


def tail_rows(norms, share):
    high, low = split(norms)
    return jnp.concatenate([high, low, jnp.zeros((TAIL - 2, share), BF16)], axis=0)


def partner(index, step, size):
    if size & (size - 1) == 0:
        return index ^ step
    return lax.rem(index + size - step, size)


def exchange(value, axis, step):
    size = lax.axis_size(axis)
    pairs = [
        ((i ^ step) if size & (size - 1) == 0 else (i + size - step) % size, i) for i in range(size)
    ]
    return lax.ppermute(value, axis, pairs)


def message_kernel(count, depth, mine, got, norms, *outs):
    half = lax.axis_index("half")
    me = lax.axis_index("row")
    rows = count * depth
    share = mine.shape[1]
    total = norms[...] + got[rows : rows + 1, :].astype(F32) + got[rows + 1 : rows + 2, :].astype(F32)
    outs[-1][...] = total
    for s in range(count):
        at = pl.ds(pl.multiple_of(destination(me, s, count) * depth, depth), depth)
        first, second = mine[at, :], got[at, :]
        swap = half == 1
        out = outs[count - 1 - s]
        out[:depth, :] = jnp.where(swap, second, first)
        out[depth : 2 * depth, :] = jnp.where(swap, first, second)
        if s:
            out[2 * depth :, :] = tail_rows(total, share)


def destination(index, step, size):
    if size & (size - 1) == 0:
        return index ^ step
    return lax.rem(index + step, size)


def scale_kernel(count, depth, *refs):
    pieces, norms, out = refs[:count][::-1], refs[count], refs[count + 1]
    me = lax.axis_index("row")
    total = norms[...]
    for s in range(1, count):
        total = total + pieces[s][2 * depth : 2 * depth + 1, :].astype(F32)
        total = total + pieces[s][2 * depth + 1 : 2 * depth + 2, :].astype(F32)
    scale = lax.rsqrt(total + 1e-06)
    for s in range(count):
        value = (pieces[s][: 2 * depth, :].astype(F32) * scale).astype(BF16)
        out[partner(me, s, count)] = value


def body(chip, vecs, poles, weights, kept, roots, order):
    row_count, col_count, halves = (lax.axis_size(a) for a in ("row", "col", "half"))
    own = roots.shape[0]
    width = order.shape[0]
    columns = poles.shape[1]
    nrows = vecs.shape[1]
    share = width // col_count
    groups = row_count * halves
    depth = nrows // groups
    direct = halves == 2 and depth % 16 == 0

    roots = roots.reshape(1, own)
    order = order.reshape(1, width)
    hbm = pl.BlockSpec(memory_space=pltpu.HBM)
    kept_bytes = 2 * nrows * columns + 4 * (2 * columns + own * (row_count + 1) + 2 * width) + SLACK
    loading = pltpu.CompilerParams(vmem_limit_bytes=VMEM_BYTES - kept_bytes - 3 * nrows * columns)
    pieces = [roots] + [exchange(roots, "row", s) for s in range(1, row_count)]
    poles, pieces[0], order, started, scaled, sums = pl.pallas_call(
        norm_kernel,
        out_shape=(
            pltpu.VMEM((1, columns), F32),
            pltpu.VMEM((1, own), F32),
            pltpu.VMEM((1, width), I32),
            pltpu.VMEM((nrows, columns), BF16),
            pltpu.VMEM((1, columns), F32),
            pltpu.VMEM((1, width), F32),
        ),
        in_specs=[hbm] * 6,
        out_specs=(VMEM,) * 6,
        scratch_shapes=[
            pltpu.VMEM((1, columns), F32),
            pltpu.VMEM((1, columns), I32),
            pltpu.SemaphoreType.DMA((5,)),
            pltpu.SemaphoreType.DMA,
        ],
        compiler_params=pltpu.CompilerParams(vmem_limit_bytes=VMEM_BYTES - kept_bytes),
        cost_estimate=pl.CostEstimate(
            flops=6 * own * columns, transcendentals=own * columns, bytes_accessed=nrows * columns
        ),
        name="norms",
    )(poles, weights, kept, roots, order, vecs)

    def panel(shift, loaded):
        loads = loaded is None
        args = (*pieces, order, poles, scaled, sums) + ((started, vecs) if loads else (loaded,))
        out = pltpu.VMEM((nrows + TAIL, share), BF16) if shift else pltpu.VMEM((share, nrows), F32)
        results = pl.pallas_call(
            functools.partial(panel_kernel, chip, row_count, shift, loads),
            out_shape=(out, pltpu.VMEM((nrows, columns), BF16)) if loads else (out,),
            in_specs=[VMEM] * (len(args) - 1) + [hbm if loads else VMEM],
            out_specs=(VMEM, VMEM) if loads else (VMEM,),
            input_output_aliases={len(args) - 2: 1} if loads else {},
            scratch_shapes=[
                pltpu.VMEM((share, LANES), F32),
                pltpu.VMEM((share, nrows), F32),
            ]
            + ([pltpu.SemaphoreType.DMA] if loads else []),
            compiler_params=loading if loads else params(16),
            cost_estimate=pl.CostEstimate(
                flops=2 * share * nrows * columns,
                transcendentals=share * columns,
                bytes_accessed=nrows * columns * 2,
            ),
            name=f"panel_{shift}",
        )(*args)
        return results if loads else (results[0], loaded)

    received = []
    loaded = None
    for shift in range(1, col_count):
        pairs = [(i, (i + shift) % col_count) for i in range(col_count)]
        message, loaded = panel(shift, loaded)
        received.append(lax.ppermute(message, "col", pairs))
    product, _ = panel(0, loaded)
    if not direct:
        full = jnp.transpose(product)
        norms = lax.dynamic_slice_in_dim(sums, lax.axis_index("col") * share, share, 1)
        for message in received:
            full = full + message[:nrows].astype(F32)
            norms = norms + jnp.sum(message[nrows : nrows + 2].astype(F32), axis=0, keepdims=True)
        norms = lax.psum(norms, ("row", "half"))
        moved = lax.all_to_all(
            full.astype(BF16).reshape(groups, depth, share),
            ("row", "half"),
            split_axis=0,
            concat_axis=0,
            tiled=True,
        )
        out = (moved.astype(F32) * lax.rsqrt(norms + 1e-06)).astype(BF16)
        return out.reshape(1, row_count, halves, depth, share)

    mine, other, norms = pl.pallas_call(
        functools.partial(add_kernel, groups),
        out_shape=(
            pltpu.VMEM((nrows // 2, share), BF16),
            pltpu.VMEM((nrows // 2 + TAIL, share), BF16),
            pltpu.VMEM((1, share), F32),
        ),
        in_specs=[VMEM] * (2 + len(received)),
        out_specs=(VMEM,) * 3,
        scratch_shapes=[pltpu.VMEM((nrows, share), F32)],
        compiler_params=params(4),
        name="add",
    )(product, sums, *received)
    got = exchange(other, "half", 1)
    shapes = [pltpu.VMEM((2 * depth + (TAIL if s else 0), share), BF16) for s in range(row_count - 1, -1, -1)]
    *messages, norms = pl.pallas_call(
        functools.partial(message_kernel, row_count, depth),
        out_shape=(*shapes, pltpu.VMEM((1, share), F32)),
        in_specs=[VMEM] * 3,
        out_specs=(VMEM,) * (row_count + 1),
        compiler_params=params(4),
        name="messages",
    )(mine, got, norms)
    landed = []
    for s in range(row_count - 1, 0, -1):
        pairs = [(i, destination_of(i, s, row_count)) for i in range(row_count)]
        landed.append(lax.ppermute(messages[row_count - 1 - s], "row", pairs))
    landed.append(messages[-1])
    out = pl.pallas_call(
        functools.partial(scale_kernel, row_count, depth),
        out_shape=jax.ShapeDtypeStruct((row_count, 2 * depth, share), BF16),
        in_specs=[VMEM] * (row_count + 1),
        out_specs=VMEM,
        compiler_params=params(4),
        name="scale",
    )(*landed, norms)
    return out.reshape(1, row_count, halves, depth, share)


def destination_of(index, step, size):
    return (index ^ step) if size & (size - 1) == 0 else (index + step) % size


def solution(mesh):
    return jax.shard_map(
        functools.partial(body, mesh.abstract_mesh),
        mesh=mesh,
        in_specs=(
            P(("grp", "half"), "row", "col"),
            P(("grp", "half"), "col"),
            P(("grp", "half"), "col"),
            P(("grp", "half"), "col"),
            P(("grp", "row")),
            P("grp"),
        ),
        out_specs=P(("grp", "row", "half"), None, None, None, "col"),
        check_vma=False,
    )
```

```python
import functools

import jax
import jax.numpy as jnp
from jax import lax
from jax.experimental import pallas as pl
from jax.experimental.pallas import tpu as pltpu
from jax.sharding import PartitionSpec as P

F32, BF16, I32 = jnp.float32, jnp.bfloat16, jnp.int32
LANES = 128
VMEM_BYTES = 67_043_328
SLACK = 32 << 10
MXU = 256
PARTS = ((0, 6), (6, 8))
TAIL = 8
VMEM = pl.BlockSpec(memory_space=pltpu.VMEM)


def params(mib):
    return pltpu.CompilerParams(vmem_limit_bytes=mib << 20)


def tile_of(size, most):
    tile = most
    while size % tile:
        tile //= 2
    return tile


def column_of(row):
    n = row.shape[1]
    sub = lax.broadcasted_iota(I32, (n, n), 0)
    lane = lax.broadcasted_iota(I32, (n, n), 1)
    return jnp.sum(jnp.where(sub == lane, row, jnp.zeros_like(row)), axis=1, keepdims=True)


def split(value):
    high = value.astype(BF16)
    return high, (value - high.astype(F32)).astype(BF16)


def part_of(source, target, span, sem):
    size = target.shape[1] // 8
    at = slice(span[0] * size, span[1] * size)
    return pltpu.make_async_copy(source.at[0, :, at], target.at[:, at], sem)


def squares(poles, scaled, theta):
    columns = poles.shape[1]
    step = tile_of(columns, 16 * LANES)

    def body(i, total):
        for j in range(step // LANES):
            at = pl.ds(pl.multiple_of(i * step + j * LANES, LANES), LANES)
            c = scaled[:, at] * (1.0 / (poles[:, at] - theta))
            total = total + c * c
        return total

    return lax.fori_loop(0, columns // step, body, jnp.zeros(theta.shape, F32))


def norm_kernel(poles, weights, kept, roots, order, vecs, *refs):
    poles_in, roots_in, order_in, vecs_in, scaled, sums = refs[:6]
    weights_in, kept_in, sem, bulk = refs[6:]
    pairs = ((poles, poles_in), (weights, weights_in), (kept, kept_in), (roots, roots_in), (order, order_in))
    small = [pltpu.make_async_copy(a, b, sem.at[i]) for i, (a, b) in enumerate(pairs)]
    for copy in small:
        copy.start()
    large = part_of(vecs, vecs_in, PARTS[0], bulk)
    large.start()
    for copy in small:
        copy.wait()
    own = roots.shape[1]
    scaled[...] = weights_in[...] * kept_in[...].astype(F32)
    theta = jnp.broadcast_to(column_of(roots_in[...]), (own, LANES))
    total = squares(poles_in, scaled, theta)
    column = jnp.sum(total, axis=1, keepdims=True)
    base = lax.axis_index("row") * own
    sub = lax.broadcasted_iota(I32, (own, order.shape[1]), 0)
    hit = (order_in[...] - base) == sub
    sums[...] = jnp.sum(jnp.where(hit, column, 0.0), axis=0, keepdims=True)
    large.wait()


def panel_kernel(chip, count, shift, loads, *refs):
    roots = refs[:count]
    if loads:
        order, poles, scaled, sums, _, source, out, vecs, theta, acc, sem = refs[count:]
        copy = part_of(source, vecs, PARTS[1], sem)
        copy.start()
    else:
        order, poles, scaled, sums, vecs, out, theta, acc = refs[count:]
    nrows = vecs.shape[0]
    share = theta.shape[0]
    own = roots[0].shape[1]
    columns = poles.shape[1]
    me = lax.axis_index("row")
    cols = lax.axis_size("col")
    target = lax.rem(lax.axis_index("col") + shift, cols)
    start = pl.multiple_of(target * share, LANES)
    for b in range(share // LANES):
        picks = column_of(order[:, pl.ds(pl.multiple_of(start + b * LANES, LANES), LANES)])
        total = jnp.zeros((LANES, 1), F32)
        for s in range(count):
            lane = lax.broadcasted_iota(I32, (LANES, roots[s].shape[1]), 1)
            lane = lane + partner(me, s, count) * own
            total = total + jnp.sum(jnp.where(picks == lane, roots[s][...], 0.0), axis=1, keepdims=True)
        theta[b * LANES : (b + 1) * LANES, :] = jnp.broadcast_to(total, (LANES, LANES))

    tile = MXU

    def run(start, stop, units):
        for t in range(start // tile, stop // tile):
            at = [slice(t * tile + j * LANES, t * tile + (j + 1) * LANES) for j in range(tile // LANES)]
            panel = [(scaled[:, c] * (1.0 / (poles[:, c] - theta[...]))).astype(BF16) for c in at]
            unit, register = t % 2, (t // 2) % 2
            right = vecs[:, t * tile : (t + 1) * tile]
            pltpu.matmul_push_rhs(right, staging_register=register, mxu_index=unit, transpose=True)
            pltpu.matmul_acc_lhs(units[unit], jnp.concatenate(panel, axis=1), load_staged_rhs=register)

    def multiply(*units):
        here = PARTS[1][0] * (columns // 8) if loads else columns
        run(0, here, units)
        if loads:
            copy.wait()
            run(here, columns, units)
        acc[...] = pltpu.matmul_pop(units[0]) + pltpu.matmul_pop(units[1])

    with jax.sharding.use_abstract_mesh(chip):
        pl.run_scoped(multiply, *(pltpu.ACC(unit)((share, nrows), F32) for unit in range(2)))
    total = acc[...]
    if shift == 0:
        out[...] = total
        return
    out[:nrows, :] = total.astype(BF16).T
    out[nrows:, :] = tail_rows(sums[:, pl.ds(start, share)], share)


def add_kernel(count, product, sums, *refs):
    received, outs, full = refs[: -count - 2], refs[-count - 2 : -1], refs[-1]
    share, nrows = product.shape
    norms = sums[:, pl.ds(pl.multiple_of(lax.axis_index("col") * share, LANES), share)]
    full[...] = product[...].T
    for ref in received:
        full[...] += ref[:nrows, :].astype(F32)
        norms = norms + ref[nrows : nrows + 1, :].astype(F32) + ref[nrows + 1 : nrows + 2, :].astype(F32)
    outs[-1][...] = norms
    me = lax.axis_index("row")
    rows = nrows // count
    for s in range(count):
        out = outs[count - 1 - s]
        at = pl.ds(pl.multiple_of(destination(me, s, count) * rows, rows), rows)
        out[:rows, :] = full[at, :].astype(BF16)
        if s:
            out[rows:, :] = tail_rows(norms, share)


def tail_rows(norms, share):
    high, low = split(norms)
    return jnp.concatenate([high, low, jnp.zeros((TAIL - 2, share), BF16)], axis=0)


def partner(index, step, size):
    if size & (size - 1) == 0:
        return index ^ step
    return lax.rem(index + size - step, size)


def exchange(value, axis, step):
    size = lax.axis_size(axis)
    pairs = [
        ((i ^ step) if size & (size - 1) == 0 else (i + size - step) % size, i) for i in range(size)
    ]
    return lax.ppermute(value, axis, pairs)


def destination(index, step, size):
    if size & (size - 1) == 0:
        return index ^ step
    return lax.rem(index + step, size)


def sort_kernel(count, depth, *refs):
    pieces, norms, mine, other, total_norms = refs[:count][::-1], *refs[count:]
    me = lax.axis_index("row")
    half = lax.axis_index("half")
    total = norms[...]
    for s in range(count):
        at = pl.ds(pl.multiple_of(partner(me, s, count) * depth, depth), depth)
        for which, ref in ((half, mine), (1 - half, other)):
            ref[at, :] = pieces[s][pl.ds(pl.multiple_of(which * depth, depth), depth), :]
        if s:
            total = total + pieces[s][2 * depth : 2 * depth + 1, :].astype(F32)
            total = total + pieces[s][2 * depth + 1 : 2 * depth + 2, :].astype(F32)
    total_norms[...] = total
    other[count * depth :, :] = tail_rows(total, mine.shape[1])


def scale_kernel(count, depth, mine, got, norms, out):
    half = lax.axis_index("half")
    rows = count * depth
    total = norms[...] + got[rows : rows + 1, :].astype(F32) + got[rows + 1 : rows + 2, :].astype(F32)
    scale = lax.rsqrt(total + 1e-06)
    for r in range(count):
        for which, ref in ((half, mine), (1 - half, got)):
            value = ref[r * depth : (r + 1) * depth, :].astype(F32) * scale
            out[r, which] = value.astype(BF16)


def body(chip, vecs, poles, weights, kept, roots, order):
    row_count, col_count, halves = (lax.axis_size(a) for a in ("row", "col", "half"))
    own = roots.shape[0]
    width = order.shape[0]
    columns = poles.shape[1]
    nrows = vecs.shape[1]
    share = width // col_count
    groups = row_count * halves
    depth = nrows // groups
    direct = halves == 2 and depth % 16 == 0

    roots = roots.reshape(1, own)
    order = order.reshape(1, width)
    hbm = pl.BlockSpec(memory_space=pltpu.HBM)
    kept_bytes = 2 * nrows * columns + 4 * (2 * columns + own * (row_count + 1) + 2 * width) + SLACK
    loading = pltpu.CompilerParams(vmem_limit_bytes=VMEM_BYTES - kept_bytes - 3 * nrows * columns)
    pieces = [roots] + [exchange(roots, "row", s) for s in range(1, row_count)]
    poles, pieces[0], order, started, scaled, sums = pl.pallas_call(
        norm_kernel,
        out_shape=(
            pltpu.VMEM((1, columns), F32),
            pltpu.VMEM((1, own), F32),
            pltpu.VMEM((1, width), I32),
            pltpu.VMEM((nrows, columns), BF16),
            pltpu.VMEM((1, columns), F32),
            pltpu.VMEM((1, width), F32),
        ),
        in_specs=[hbm] * 6,
        out_specs=(VMEM,) * 6,
        scratch_shapes=[
            pltpu.VMEM((1, columns), F32),
            pltpu.VMEM((1, columns), I32),
            pltpu.SemaphoreType.DMA((5,)),
            pltpu.SemaphoreType.DMA,
        ],
        compiler_params=pltpu.CompilerParams(vmem_limit_bytes=VMEM_BYTES - kept_bytes),
        cost_estimate=pl.CostEstimate(
            flops=6 * own * columns, transcendentals=own * columns, bytes_accessed=nrows * columns
        ),
        name="norms",
    )(poles, weights, kept, roots, order, vecs)

    def panel(shift, loaded):
        loads = loaded is None
        args = (*pieces, order, poles, scaled, sums) + ((started, vecs) if loads else (loaded,))
        out = pltpu.VMEM((nrows + TAIL, share), BF16) if shift else pltpu.VMEM((share, nrows), F32)
        results = pl.pallas_call(
            functools.partial(panel_kernel, chip, row_count, shift, loads),
            out_shape=(out, pltpu.VMEM((nrows, columns), BF16)) if loads else (out,),
            in_specs=[VMEM] * (len(args) - 1) + [hbm if loads else VMEM],
            out_specs=(VMEM, VMEM) if loads else (VMEM,),
            input_output_aliases={len(args) - 2: 1} if loads else {},
            scratch_shapes=[
                pltpu.VMEM((share, LANES), F32),
                pltpu.VMEM((share, nrows), F32),
            ]
            + ([pltpu.SemaphoreType.DMA] if loads else []),
            compiler_params=loading if loads else params(16),
            cost_estimate=pl.CostEstimate(
                flops=2 * share * nrows * columns,
                transcendentals=share * columns,
                bytes_accessed=nrows * columns * 2,
            ),
            name=f"panel_{shift}",
        )(*args)
        return results if loads else (results[0], loaded)

    received = []
    loaded = None
    for shift in range(1, col_count):
        pairs = [(i, (i + shift) % col_count) for i in range(col_count)]
        message, loaded = panel(shift, loaded)
        received.append(lax.ppermute(message, "col", pairs))
    product, _ = panel(0, loaded)
    if not direct:
        full = jnp.transpose(product)
        norms = lax.dynamic_slice_in_dim(sums, lax.axis_index("col") * share, share, 1)
        for message in received:
            full = full + message[:nrows].astype(F32)
            norms = norms + jnp.sum(message[nrows : nrows + 2].astype(F32), axis=0, keepdims=True)
        norms = lax.psum(norms, ("row", "half"))
        moved = lax.all_to_all(
            full.astype(BF16).reshape(groups, depth, share),
            ("row", "half"),
            split_axis=0,
            concat_axis=0,
            tiled=True,
        )
        out = (moved.astype(F32) * lax.rsqrt(norms + 1e-06)).astype(BF16)
        return out.reshape(1, row_count, halves, depth, share)

    shapes = [pltpu.VMEM((2 * depth + (TAIL if s else 0), share), BF16) for s in range(row_count - 1, -1, -1)]
    *messages, norms = pl.pallas_call(
        functools.partial(add_kernel, row_count),
        out_shape=(*shapes, pltpu.VMEM((1, share), F32)),
        in_specs=[VMEM] * (2 + len(received)),
        out_specs=(VMEM,) * (row_count + 1),
        scratch_shapes=[pltpu.VMEM((nrows, share), F32)],
        compiler_params=params(4),
        name="add",
    )(product, sums, *received)
    landed = []
    for s in range(row_count - 1, 0, -1):
        pairs = [(i, destination_of(i, s, row_count)) for i in range(row_count)]
        landed.append(lax.ppermute(messages[row_count - 1 - s], "row", pairs))
    landed.append(messages[-1])
    rows = row_count * depth
    mine, other, norms = pl.pallas_call(
        functools.partial(sort_kernel, row_count, depth),
        out_shape=(
            pltpu.VMEM((rows, share), BF16),
            pltpu.VMEM((rows + TAIL, share), BF16),
            pltpu.VMEM((1, share), F32),
        ),
        in_specs=[VMEM] * (row_count + 1),
        out_specs=(VMEM,) * 3,
        compiler_params=params(4),
        name="sort",
    )(*landed, norms)
    got = exchange(other, "half", 1)
    out = pl.pallas_call(
        functools.partial(scale_kernel, row_count, depth),
        out_shape=jax.ShapeDtypeStruct((row_count, halves, depth, share), BF16),
        in_specs=[VMEM] * 3,
        out_specs=VMEM,
        compiler_params=params(4),
        name="scale",
    )(mine, got, norms)
    return out.reshape(1, row_count, halves, depth, share)


def destination_of(index, step, size):
    return (index ^ step) if size & (size - 1) == 0 else (index + step) % size


def solution(mesh):
    return jax.shard_map(
        functools.partial(body, mesh.abstract_mesh),
        mesh=mesh,
        in_specs=(
            P(("grp", "half"), "row", "col"),
            P(("grp", "half"), "col"),
            P(("grp", "half"), "col"),
            P(("grp", "half"), "col"),
            P(("grp", "row")),
            P("grp"),
        ),
        out_specs=P(("grp", "row", "half"), None, None, None, "col"),
        check_vma=False,
    )
```

```python
import functools

import jax
import jax.numpy as jnp
from jax import lax
from jax.experimental import pallas as pl
from jax.experimental.pallas import tpu as pltpu
from jax.sharding import PartitionSpec as P

F32, BF16, I32 = jnp.float32, jnp.bfloat16, jnp.int32
LANES = 128
VMEM_BYTES = 67_043_328
SLACK = 32 << 10
MXU = 256
PARTS = ((0, 6), (6, 8))
TAIL = 8
VMEM = pl.BlockSpec(memory_space=pltpu.VMEM)


def params(mib):
    return pltpu.CompilerParams(vmem_limit_bytes=mib << 20)


def tile_of(size, most):
    tile = most
    while size % tile:
        tile //= 2
    return tile


def column_of(row):
    n = row.shape[1]
    sub = lax.broadcasted_iota(I32, (n, n), 0)
    lane = lax.broadcasted_iota(I32, (n, n), 1)
    return jnp.sum(jnp.where(sub == lane, row, jnp.zeros_like(row)), axis=1, keepdims=True)


def split(value):
    high = value.astype(BF16)
    return high, (value - high.astype(F32)).astype(BF16)


def part_of(source, target, span, sem):
    size = target.shape[1] // 8
    at = slice(span[0] * size, span[1] * size)
    return pltpu.make_async_copy(source.at[0, :, at], target.at[:, at], sem)


def squares(poles, scaled, theta):
    columns = poles.shape[1]
    step = tile_of(columns, 16 * LANES)

    def body(i, total):
        for j in range(step // LANES):
            at = pl.ds(pl.multiple_of(i * step + j * LANES, LANES), LANES)
            c = scaled[:, at] * (1.0 / (poles[:, at] - theta))
            total = total + c * c
        return total

    return lax.fori_loop(0, columns // step, body, jnp.zeros(theta.shape, F32))


def norm_kernel(poles, weights, kept, roots, order, vecs, *refs):
    poles_in, roots_in, order_in, vecs_in, scaled, sums = refs[:6]
    weights_in, kept_in, sem, bulk = refs[6:]
    pairs = ((poles, poles_in), (weights, weights_in), (kept, kept_in), (roots, roots_in), (order, order_in))
    small = [pltpu.make_async_copy(a, b, sem.at[i]) for i, (a, b) in enumerate(pairs)]
    for copy in small:
        copy.start()
    large = part_of(vecs, vecs_in, PARTS[0], bulk)
    large.start()
    for copy in small:
        copy.wait()
    own = roots.shape[1]
    scaled[...] = weights_in[...] * kept_in[...].astype(F32)
    theta = jnp.broadcast_to(column_of(roots_in[...]), (own, LANES))
    total = squares(poles_in, scaled, theta)
    column = jnp.sum(total, axis=1, keepdims=True)
    base = lax.axis_index("row") * own
    sub = lax.broadcasted_iota(I32, (own, order.shape[1]), 0)
    hit = (order_in[...] - base) == sub
    sums[...] = jnp.sum(jnp.where(hit, column, 0.0), axis=0, keepdims=True)
    large.wait()


def panel_kernel(chip, count, shift, loads, *refs):
    roots = refs[:count]
    if loads:
        order, poles, scaled, sums, _, source, out, vecs, theta, acc, sem = refs[count:]
        copy = part_of(source, vecs, PARTS[1], sem)
        copy.start()
    else:
        order, poles, scaled, sums, vecs, out, theta, acc = refs[count:]
    nrows = vecs.shape[0]
    share = theta.shape[0]
    own = roots[0].shape[1]
    columns = poles.shape[1]
    me = lax.axis_index("row")
    cols = lax.axis_size("col")
    target = lax.rem(lax.axis_index("col") + shift, cols)
    start = pl.multiple_of(target * share, LANES)
    for b in range(share // LANES):
        picks = column_of(order[:, pl.ds(pl.multiple_of(start + b * LANES, LANES), LANES)])
        total = jnp.zeros((LANES, 1), F32)
        for s, step in enumerate(turns(count)):
            lane = lax.broadcasted_iota(I32, (LANES, roots[s].shape[1]), 1)
            lane = lane + partner(me, step, count) * own
            total = total + jnp.sum(jnp.where(picks == lane, roots[s][...], 0.0), axis=1, keepdims=True)
        theta[b * LANES : (b + 1) * LANES, :] = jnp.broadcast_to(total, (LANES, LANES))

    tile = MXU

    def run(start, stop, units):
        for t in range(start // tile, stop // tile):
            at = [slice(t * tile + j * LANES, t * tile + (j + 1) * LANES) for j in range(tile // LANES)]
            panel = [(scaled[:, c] * (1.0 / (poles[:, c] - theta[...]))).astype(BF16) for c in at]
            unit, register = t % 2, (t // 2) % 2
            right = vecs[:, t * tile : (t + 1) * tile]
            pltpu.matmul_push_rhs(right, staging_register=register, mxu_index=unit, transpose=True)
            pltpu.matmul_acc_lhs(units[unit], jnp.concatenate(panel, axis=1), load_staged_rhs=register)

    def multiply(*units):
        here = PARTS[1][0] * (columns // 8) if loads else columns
        run(0, here, units)
        if loads:
            copy.wait()
            run(here, columns, units)
        acc[...] = pltpu.matmul_pop(units[0]) + pltpu.matmul_pop(units[1])

    with jax.sharding.use_abstract_mesh(chip):
        pl.run_scoped(multiply, *(pltpu.ACC(unit)((share, nrows), F32) for unit in range(2)))
    total = acc[...]
    if shift == 0:
        out[...] = total
        return
    out[:nrows, :] = total.astype(BF16).T
    out[nrows:, :] = tail_rows(sums[:, pl.ds(start, share)], share)


def add_kernel(count, product, sums, *refs):
    received, outs, full = refs[: -count - 2], refs[-count - 2 : -1], refs[-1]
    share, nrows = product.shape
    norms = sums[:, pl.ds(pl.multiple_of(lax.axis_index("col") * share, LANES), share)]
    full[...] = product[...].T
    for ref in received:
        full[...] += ref[:nrows, :].astype(F32)
        norms = norms + ref[nrows : nrows + 1, :].astype(F32) + ref[nrows + 1 : nrows + 2, :].astype(F32)
    outs[-1][...] = norms
    me = lax.axis_index("row")
    rows = nrows // count
    for s in range(count):
        out = outs[count - 1 - s]
        at = pl.ds(pl.multiple_of(destination(me, s, count) * rows, rows), rows)
        out[:rows, :] = full[at, :].astype(BF16)
        if s:
            out[rows:, :] = tail_rows(norms, share)


def tail_rows(norms, share):
    high, low = split(norms)
    return jnp.concatenate([high, low, jnp.zeros((TAIL - 2, share), BF16)], axis=0)


def turns(count):
    return (0, 1, 3, 2) if count == 4 else tuple(range(count))


def partner(index, step, size):
    if size & (size - 1) == 0:
        return index ^ step
    return lax.rem(index + size - step, size)


def exchange(value, axis, step):
    size = lax.axis_size(axis)
    pairs = [
        ((i ^ step) if size & (size - 1) == 0 else (i + size - step) % size, i) for i in range(size)
    ]
    return lax.ppermute(value, axis, pairs)


def destination(index, step, size):
    if size & (size - 1) == 0:
        return index ^ step
    return lax.rem(index + step, size)


def sort_kernel(count, depth, *refs):
    pieces, norms, mine, other, total_norms = refs[:count][::-1], *refs[count:]
    me = lax.axis_index("row")
    half = lax.axis_index("half")
    total = norms[...]
    for s in range(count):
        at = pl.ds(pl.multiple_of(partner(me, s, count) * depth, depth), depth)
        for which, ref in ((half, mine), (1 - half, other)):
            ref[at, :] = pieces[s][pl.ds(pl.multiple_of(which * depth, depth), depth), :]
        if s:
            total = total + pieces[s][2 * depth : 2 * depth + 1, :].astype(F32)
            total = total + pieces[s][2 * depth + 1 : 2 * depth + 2, :].astype(F32)
    total_norms[...] = total
    other[count * depth :, :] = tail_rows(total, mine.shape[1])


def scale_kernel(count, depth, mine, got, norms, out):
    half = lax.axis_index("half")
    rows = count * depth
    total = norms[...] + got[rows : rows + 1, :].astype(F32) + got[rows + 1 : rows + 2, :].astype(F32)
    scale = lax.rsqrt(total + 1e-06)
    for r in range(count):
        for which, ref in ((half, mine), (1 - half, got)):
            value = ref[r * depth : (r + 1) * depth, :].astype(F32) * scale
            out[r, which] = value.astype(BF16)


def body(chip, vecs, poles, weights, kept, roots, order):
    row_count, col_count, halves = (lax.axis_size(a) for a in ("row", "col", "half"))
    own = roots.shape[0]
    width = order.shape[0]
    columns = poles.shape[1]
    nrows = vecs.shape[1]
    share = width // col_count
    groups = row_count * halves
    depth = nrows // groups
    direct = halves == 2 and depth % 16 == 0

    roots = roots.reshape(1, own)
    order = order.reshape(1, width)
    hbm = pl.BlockSpec(memory_space=pltpu.HBM)
    kept_bytes = 2 * nrows * columns + 4 * (2 * columns + own * (row_count + 1) + 2 * width) + SLACK
    loading = pltpu.CompilerParams(vmem_limit_bytes=VMEM_BYTES - kept_bytes - 3 * nrows * columns)
    steps = turns(row_count)
    pieces = [None] + [exchange(roots, "row", s) for s in steps[1:]]
    poles, pieces[0], order, started, scaled, sums = pl.pallas_call(
        norm_kernel,
        out_shape=(
            pltpu.VMEM((1, columns), F32),
            pltpu.VMEM((1, own), F32),
            pltpu.VMEM((1, width), I32),
            pltpu.VMEM((nrows, columns), BF16),
            pltpu.VMEM((1, columns), F32),
            pltpu.VMEM((1, width), F32),
        ),
        in_specs=[hbm] * 6,
        out_specs=(VMEM,) * 6,
        scratch_shapes=[
            pltpu.VMEM((1, columns), F32),
            pltpu.VMEM((1, columns), I32),
            pltpu.SemaphoreType.DMA((5,)),
            pltpu.SemaphoreType.DMA,
        ],
        compiler_params=pltpu.CompilerParams(vmem_limit_bytes=VMEM_BYTES - kept_bytes),
        cost_estimate=pl.CostEstimate(
            flops=6 * own * columns, transcendentals=own * columns, bytes_accessed=nrows * columns
        ),
        name="norms",
    )(poles, weights, kept, roots, order, vecs)

    def panel(shift, loaded):
        loads = loaded is None
        args = (*pieces, order, poles, scaled, sums) + ((started, vecs) if loads else (loaded,))
        out = pltpu.VMEM((nrows + TAIL, share), BF16) if shift else pltpu.VMEM((share, nrows), F32)
        results = pl.pallas_call(
            functools.partial(panel_kernel, chip, row_count, shift, loads),
            out_shape=(out, pltpu.VMEM((nrows, columns), BF16)) if loads else (out,),
            in_specs=[VMEM] * (len(args) - 1) + [hbm if loads else VMEM],
            out_specs=(VMEM, VMEM) if loads else (VMEM,),
            input_output_aliases={len(args) - 2: 1} if loads else {},
            scratch_shapes=[
                pltpu.VMEM((share, LANES), F32),
                pltpu.VMEM((share, nrows), F32),
            ]
            + ([pltpu.SemaphoreType.DMA] if loads else []),
            compiler_params=loading if loads else params(16),
            cost_estimate=pl.CostEstimate(
                flops=2 * share * nrows * columns,
                transcendentals=share * columns,
                bytes_accessed=nrows * columns * 2,
            ),
            name=f"panel_{shift}",
        )(*args)
        return results if loads else (results[0], loaded)

    received = []
    loaded = None
    for shift in range(1, col_count):
        pairs = [(i, (i + shift) % col_count) for i in range(col_count)]
        message, loaded = panel(shift, loaded)
        received.append(lax.ppermute(message, "col", pairs))
    product, _ = panel(0, loaded)
    if not direct:
        full = jnp.transpose(product)
        norms = lax.dynamic_slice_in_dim(sums, lax.axis_index("col") * share, share, 1)
        for message in received:
            full = full + message[:nrows].astype(F32)
            norms = norms + jnp.sum(message[nrows : nrows + 2].astype(F32), axis=0, keepdims=True)
        norms = lax.psum(norms, ("row", "half"))
        moved = lax.all_to_all(
            full.astype(BF16).reshape(groups, depth, share),
            ("row", "half"),
            split_axis=0,
            concat_axis=0,
            tiled=True,
        )
        out = (moved.astype(F32) * lax.rsqrt(norms + 1e-06)).astype(BF16)
        return out.reshape(1, row_count, halves, depth, share)

    shapes = [pltpu.VMEM((2 * depth + (TAIL if s else 0), share), BF16) for s in range(row_count - 1, -1, -1)]
    *messages, norms = pl.pallas_call(
        functools.partial(add_kernel, row_count),
        out_shape=(*shapes, pltpu.VMEM((1, share), F32)),
        in_specs=[VMEM] * (2 + len(received)),
        out_specs=(VMEM,) * (row_count + 1),
        scratch_shapes=[pltpu.VMEM((nrows, share), F32)],
        compiler_params=params(4),
        name="add",
    )(product, sums, *received)
    landed = []
    for s in range(row_count - 1, 0, -1):
        pairs = [(i, destination_of(i, s, row_count)) for i in range(row_count)]
        landed.append(lax.ppermute(messages[row_count - 1 - s], "row", pairs))
    landed.append(messages[-1])
    rows = row_count * depth
    mine, other, norms = pl.pallas_call(
        functools.partial(sort_kernel, row_count, depth),
        out_shape=(
            pltpu.VMEM((rows, share), BF16),
            pltpu.VMEM((rows + TAIL, share), BF16),
            pltpu.VMEM((1, share), F32),
        ),
        in_specs=[VMEM] * (row_count + 1),
        out_specs=(VMEM,) * 3,
        compiler_params=params(4),
        name="sort",
    )(*landed, norms)
    got = exchange(other, "half", 1)
    out = pl.pallas_call(
        functools.partial(scale_kernel, row_count, depth),
        out_shape=jax.ShapeDtypeStruct((row_count, halves, depth, share), BF16),
        in_specs=[VMEM] * 3,
        out_specs=VMEM,
        compiler_params=params(4),
        name="scale",
    )(mine, got, norms)
    return out.reshape(1, row_count, halves, depth, share)


def destination_of(index, step, size):
    return (index ^ step) if size & (size - 1) == 0 else (index + step) % size


def solution(mesh):
    return jax.shard_map(
        functools.partial(body, mesh.abstract_mesh),
        mesh=mesh,
        in_specs=(
            P(("grp", "half"), "row", "col"),
            P(("grp", "half"), "col"),
            P(("grp", "half"), "col"),
            P(("grp", "half"), "col"),
            P(("grp", "row")),
            P("grp"),
        ),
        out_specs=P(("grp", "row", "half"), None, None, None, "col"),
        check_vma=False,
    )
```

```python
import functools

import jax
import jax.numpy as jnp
from jax import lax
from jax.experimental import pallas as pl
from jax.experimental.pallas import tpu as pltpu
from jax.sharding import PartitionSpec as P

F32, BF16, I32 = jnp.float32, jnp.bfloat16, jnp.int32
LANES = 128
VMEM_BYTES = 67_043_328
SLACK = 32 << 10
MXU = 256
PARTS = ((0, 10), (10, 13), (13, 16))
TAIL = 8
VMEM = pl.BlockSpec(memory_space=pltpu.VMEM)


def params(mib):
    return pltpu.CompilerParams(vmem_limit_bytes=mib << 20)


def tile_of(size, most):
    tile = most
    while size % tile:
        tile //= 2
    return tile


def column_of(row):
    n = row.shape[1]
    sub = lax.broadcasted_iota(I32, (n, n), 0)
    lane = lax.broadcasted_iota(I32, (n, n), 1)
    return jnp.sum(jnp.where(sub == lane, row, jnp.zeros_like(row)), axis=1, keepdims=True)


def split(value):
    high = value.astype(BF16)
    return high, (value - high.astype(F32)).astype(BF16)


def part_of(source, target, span, sem):
    size = target.shape[1] // 16
    at = slice(span[0] * size, span[1] * size)
    return pltpu.make_async_copy(source.at[0, :, at], target.at[:, at], sem)


def squares(poles, scaled, theta):
    columns = poles.shape[1]
    step = tile_of(columns, 16 * LANES)

    def body(i, total):
        for j in range(step // LANES):
            at = pl.ds(pl.multiple_of(i * step + j * LANES, LANES), LANES)
            c = scaled[:, at] * (1.0 / (poles[:, at] - theta))
            total = total + c * c
        return total

    return lax.fori_loop(0, columns // step, body, jnp.zeros(theta.shape, F32))


def norm_kernel(poles, weights, kept, roots, order, vecs, *refs):
    poles_in, roots_in, order_in, vecs_in, scaled, sums = refs[:6]
    weights_in, kept_in, sem, bulk = refs[6:]
    pairs = ((poles, poles_in), (weights, weights_in), (kept, kept_in), (roots, roots_in), (order, order_in))
    small = [pltpu.make_async_copy(a, b, sem.at[i]) for i, (a, b) in enumerate(pairs)]
    for copy in small:
        copy.start()
    large = part_of(vecs, vecs_in, PARTS[0], bulk)
    large.start()
    for copy in small:
        copy.wait()
    own = roots.shape[1]
    scaled[...] = weights_in[...] * kept_in[...].astype(F32)
    theta = jnp.broadcast_to(column_of(roots_in[...]), (own, LANES))
    total = squares(poles_in, scaled, theta)
    column = jnp.sum(total, axis=1, keepdims=True)
    base = lax.axis_index("row") * own
    sub = lax.broadcasted_iota(I32, (own, order.shape[1]), 0)
    hit = (order_in[...] - base) == sub
    sums[...] = jnp.sum(jnp.where(hit, column, 0.0), axis=0, keepdims=True)
    large.wait()


def panel_kernel(chip, count, shift, loads, *refs):
    roots = refs[:count]
    if loads:
        order, poles, scaled, sums, _, source, out, vecs, theta, acc, sem = refs[count:]
        copies = [part_of(source, vecs, span, sem.at[i]) for i, span in enumerate(PARTS[1:])]
        for copy in copies:
            copy.start()
    else:
        order, poles, scaled, sums, vecs, out, theta, acc = refs[count:]
    nrows = vecs.shape[0]
    share = theta.shape[0]
    own = roots[0].shape[1]
    columns = poles.shape[1]
    me = lax.axis_index("row")
    cols = lax.axis_size("col")
    target = lax.rem(lax.axis_index("col") + shift, cols)
    start = pl.multiple_of(target * share, LANES)
    for b in range(share // LANES):
        picks = column_of(order[:, pl.ds(pl.multiple_of(start + b * LANES, LANES), LANES)])
        lane = lax.broadcasted_iota(I32, (LANES, own), 1)
        total = jnp.zeros((LANES, own), F32)
        for s, step in enumerate(turns(count)):
            total = jnp.where(picks - partner(me, step, count) * own == lane, roots[s][...], total)
        theta[b * LANES : (b + 1) * LANES, :] = jnp.broadcast_to(
            jnp.sum(total, axis=1, keepdims=True), (LANES, LANES)
        )

    tile = MXU

    def run(start, stop, units):
        for t in range(start // tile, stop // tile):
            at = [slice(t * tile + j * LANES, t * tile + (j + 1) * LANES) for j in range(tile // LANES)]
            panel = [(scaled[:, c] * (1.0 / (poles[:, c] - theta[...]))).astype(BF16) for c in at]
            unit, register = t % 2, (t // 2) % 2
            right = vecs[:, t * tile : (t + 1) * tile]
            pltpu.matmul_push_rhs(right, staging_register=register, mxu_index=unit, transpose=True)
            pltpu.matmul_acc_lhs(units[unit], jnp.concatenate(panel, axis=1), load_staged_rhs=register)

    def multiply(*units):
        for i, span in enumerate(PARTS):
            if loads and i:
                copies[i - 1].wait()
            run(span[0] * (columns // 16), span[1] * (columns // 16), units)
        acc[...] = pltpu.matmul_pop(units[0]) + pltpu.matmul_pop(units[1])

    with jax.sharding.use_abstract_mesh(chip):
        pl.run_scoped(multiply, *(pltpu.ACC(unit)((share, nrows), F32) for unit in range(2)))
    total = acc[...]
    if shift == 0:
        out[...] = total
        return
    out[:share, :] = total.astype(BF16)
    out[share:, :share] = tail_rows(sums[:, pl.ds(start, share)], share)


def add_kernel(count, product, sums, *refs):
    received, outs, full = refs[: -count - 2], refs[-count - 2 : -1], refs[-1]
    share, nrows = product.shape
    norms = sums[:, pl.ds(pl.multiple_of(lax.axis_index("col") * share, LANES), share)]
    total = product[...]
    for ref in received:
        total = total + ref[:share, :].astype(F32)
        norms = norms + ref[share : share + 1, :share].astype(F32) + ref[share + 1 : share + 2, :share].astype(F32)
    full[...] = total.T
    outs[-1][...] = norms
    me = lax.axis_index("row")
    rows = nrows // count
    for s in range(count):
        out = outs[count - 1 - s]
        at = pl.ds(pl.multiple_of(destination(me, s, count) * rows, rows), rows)
        out[:rows, :] = full[at, :].astype(BF16)
        if s:
            out[rows:, :] = tail_rows(norms, share)


def tail_rows(norms, share):
    high, low = split(norms)
    return jnp.concatenate([high, low, jnp.zeros((TAIL - 2, share), BF16)], axis=0)


def turns(count):
    return (0, 1, 3, 2) if count == 4 else tuple(range(count))


def partner(index, step, size):
    if size & (size - 1) == 0:
        return index ^ step
    return lax.rem(index + size - step, size)


def exchange(value, axis, step):
    size = lax.axis_size(axis)
    pairs = [
        ((i ^ step) if size & (size - 1) == 0 else (i + size - step) % size, i) for i in range(size)
    ]
    return lax.ppermute(value, axis, pairs)


def destination(index, step, size):
    if size & (size - 1) == 0:
        return index ^ step
    return lax.rem(index + step, size)


def sort_kernel(count, depth, *refs):
    pieces, norms, mine, other, total_norms = refs[:count][::-1], *refs[count:]
    me = lax.axis_index("row")
    half = lax.axis_index("half")
    total = norms[...]
    for s in range(count):
        at = pl.ds(pl.multiple_of(partner(me, s, count) * depth, depth), depth)
        for which, ref in ((half, mine), (1 - half, other)):
            ref[at, :] = pieces[s][pl.ds(pl.multiple_of(which * depth, depth), depth), :]
        if s:
            total = total + pieces[s][2 * depth : 2 * depth + 1, :].astype(F32)
            total = total + pieces[s][2 * depth + 1 : 2 * depth + 2, :].astype(F32)
    total_norms[...] = total
    other[count * depth :, :] = tail_rows(total, mine.shape[1])


def scale_kernel(count, depth, mine, got, norms, out):
    half = lax.axis_index("half")
    rows = count * depth
    total = norms[...] + got[rows : rows + 1, :].astype(F32) + got[rows + 1 : rows + 2, :].astype(F32)
    scale = lax.rsqrt(total + 1e-06)
    for r in range(count):
        for which, ref in ((half, mine), (1 - half, got)):
            value = ref[r * depth : (r + 1) * depth, :].astype(F32) * scale
            out[r, which] = value.astype(BF16)


def body(chip, vecs, poles, weights, kept, roots, order):
    row_count, col_count, halves = (lax.axis_size(a) for a in ("row", "col", "half"))
    own = roots.shape[0]
    width = order.shape[0]
    columns = poles.shape[1]
    nrows = vecs.shape[1]
    share = width // col_count
    groups = row_count * halves
    depth = nrows // groups
    direct = halves == 2 and depth % 16 == 0

    roots = roots.reshape(1, own)
    order = order.reshape(1, width)
    hbm = pl.BlockSpec(memory_space=pltpu.HBM)
    kept_bytes = 2 * nrows * columns + 4 * (2 * columns + own * (row_count + 1) + 2 * width) + SLACK
    loading = pltpu.CompilerParams(vmem_limit_bytes=VMEM_BYTES - kept_bytes - 3 * nrows * columns)
    steps = turns(row_count)
    pieces = [None] + [exchange(roots, "row", s) for s in steps[1:]]
    poles, pieces[0], order, started, scaled, sums = pl.pallas_call(
        norm_kernel,
        out_shape=(
            pltpu.VMEM((1, columns), F32),
            pltpu.VMEM((1, own), F32),
            pltpu.VMEM((1, width), I32),
            pltpu.VMEM((nrows, columns), BF16),
            pltpu.VMEM((1, columns), F32),
            pltpu.VMEM((1, width), F32),
        ),
        in_specs=[hbm] * 6,
        out_specs=(VMEM,) * 6,
        scratch_shapes=[
            pltpu.VMEM((1, columns), F32),
            pltpu.VMEM((1, columns), I32),
            pltpu.SemaphoreType.DMA((5,)),
            pltpu.SemaphoreType.DMA,
        ],
        compiler_params=pltpu.CompilerParams(vmem_limit_bytes=VMEM_BYTES - kept_bytes),
        cost_estimate=pl.CostEstimate(
            flops=6 * own * columns, transcendentals=own * columns, bytes_accessed=nrows * columns
        ),
        name="norms",
    )(poles, weights, kept, roots, order, vecs)

    def panel(shift, loaded):
        loads = loaded is None
        args = (*pieces, order, poles, scaled, sums) + ((started, vecs) if loads else (loaded,))
        out = pltpu.VMEM((share + TAIL, nrows), BF16) if shift else pltpu.VMEM((share, nrows), F32)
        results = pl.pallas_call(
            functools.partial(panel_kernel, chip, row_count, shift, loads),
            out_shape=(out, pltpu.VMEM((nrows, columns), BF16)) if loads else (out,),
            in_specs=[VMEM] * (len(args) - 1) + [hbm if loads else VMEM],
            out_specs=(VMEM, VMEM) if loads else (VMEM,),
            input_output_aliases={len(args) - 2: 1} if loads else {},
            scratch_shapes=[
                pltpu.VMEM((share, LANES), F32),
                pltpu.VMEM((share, nrows), F32),
            ]
            + ([pltpu.SemaphoreType.DMA((2,))] if loads else []),
            compiler_params=loading if loads else params(16),
            cost_estimate=pl.CostEstimate(
                flops=2 * share * nrows * columns,
                transcendentals=share * columns,
                bytes_accessed=nrows * columns * 2,
            ),
            name=f"panel_{shift}",
        )(*args)
        return results if loads else (results[0], loaded)

    received = []
    loaded = None
    for shift in range(1, col_count):
        pairs = [(i, (i + shift) % col_count) for i in range(col_count)]
        message, loaded = panel(shift, loaded)
        received.append(lax.ppermute(message, "col", pairs))
    product, _ = panel(0, loaded)
    if not direct:
        full = product
        norms = lax.dynamic_slice_in_dim(sums, lax.axis_index("col") * share, share, 1)
        for message in received:
            full = full + message[:share].astype(F32)
            norms = norms + jnp.sum(message[share : share + 2, :share].astype(F32), axis=0, keepdims=True)
        norms = lax.psum(norms, ("row", "half"))
        moved = lax.all_to_all(
            jnp.transpose(full.astype(BF16)).reshape(groups, depth, share),
            ("row", "half"),
            split_axis=0,
            concat_axis=0,
            tiled=True,
        )
        out = (moved.astype(F32) * lax.rsqrt(norms + 1e-06)).astype(BF16)
        return out.reshape(1, row_count, halves, depth, share)

    shapes = [pltpu.VMEM((2 * depth + (TAIL if s else 0), share), BF16) for s in range(row_count - 1, -1, -1)]
    *messages, norms = pl.pallas_call(
        functools.partial(add_kernel, row_count),
        out_shape=(*shapes, pltpu.VMEM((1, share), F32)),
        in_specs=[VMEM] * (2 + len(received)),
        out_specs=(VMEM,) * (row_count + 1),
        scratch_shapes=[pltpu.VMEM((nrows, share), F32)],
        compiler_params=params(4),
        name="add",
    )(product, sums, *received)
    landed = []
    for s in range(row_count - 1, 0, -1):
        pairs = [(i, destination_of(i, s, row_count)) for i in range(row_count)]
        landed.append(lax.ppermute(messages[row_count - 1 - s], "row", pairs))
    landed.append(messages[-1])
    rows = row_count * depth
    mine, other, norms = pl.pallas_call(
        functools.partial(sort_kernel, row_count, depth),
        out_shape=(
            pltpu.VMEM((rows, share), BF16),
            pltpu.VMEM((rows + TAIL, share), BF16),
            pltpu.VMEM((1, share), F32),
        ),
        in_specs=[VMEM] * (row_count + 1),
        out_specs=(VMEM,) * 3,
        compiler_params=params(4),
        name="sort",
    )(*landed, norms)
    got = exchange(other, "half", 1)
    out = pl.pallas_call(
        functools.partial(scale_kernel, row_count, depth),
        out_shape=jax.ShapeDtypeStruct((row_count, halves, depth, share), BF16),
        in_specs=[VMEM] * 3,
        out_specs=VMEM,
        compiler_params=params(4),
        name="scale",
    )(mine, got, norms)
    return out.reshape(1, row_count, halves, depth, share)


def destination_of(index, step, size):
    return (index ^ step) if size & (size - 1) == 0 else (index + step) % size


def solution(mesh):
    return jax.shard_map(
        functools.partial(body, mesh.abstract_mesh),
        mesh=mesh,
        in_specs=(
            P(("grp", "half"), "row", "col"),
            P(("grp", "half"), "col"),
            P(("grp", "half"), "col"),
            P(("grp", "half"), "col"),
            P(("grp", "row")),
            P("grp"),
        ),
        out_specs=P(("grp", "row", "half"), None, None, None, "col"),
        check_vma=False,
    )
```
